512 devices in a mesh: bunch: 32 (over y, x), tile: 16 (over z, core).
Axes of the slice: x: 4, y: 8, z: 8, core: 2. Of those that a mesh axis runs over, the one named last changes fastest.
Arguments:
- cell_index: int32 [2, 32, 2, 16384], P(None, 'bunch', None, 'tile'), may hold values from 0 to 255
- charges: bfloat16 [2, 32, 16384], P(None, 'bunch', 'tile'), may hold values from 0.5 to 2
- momenta: float32 [2, 32, 2, 16384], P(None, 'bunch', None, 'tile'), may hold values from -6 to 6
- fill_pattern: int32 [2, 32], P(None, 'bunch'), may hold values 0 or 1
- encounters: int32 [4, 2, 2, 32], P(None, None, None, 'bunch'), may hold values 0 or 1
- green_spectrum: float32 [256, 256], P(None, 'tile'), may hold values from 0.5 to 4
- stop_gain: float32 [4], replicated, may hold values from 0.5 to 2
- parasitic_gain: float32 [4], replicated, may hold values from 0.25 to 1
Outputs:
- kicked: float32 [2, 32, 2, 16384], P(None, 'bunch', None, 'tile')
The draws below stay inside these ranges and needn't reach their ends.
All inputs are finite; a program needn't handle non-finite values. No bound on the sum of `fill_pattern` or of `encounters` on one device may be relied on, other than what follows from the above.
Results may differ from the reference program's by a relative error of at most 0.0037.
Values may be sent and summed in bfloat16 or wider, within the bound.
A program may use at most 128 MiB of HBM per device.

```python
import math
import jax
import jax.numpy as jnp
from jax import lax

GRID = 256
STOPS = 4
OFFSET_CELLS = 32
BUN_DEV = 1
BUNCHES = 32
PARTS_SIZE = 16384


def set_ends(array, stream_key, least, largest):
    index_at = [jax.random.randint(jax.random.fold_in(stream_key, axis), (), 0, length) for axis, length in enumerate(array.shape)]
    widest = array.shape.index(max(array.shape))
    next_to = index_at[:widest] + [(index_at[widest] + 1) % array.shape[widest]] + index_at[widest + 1:]
    return array.at[tuple(index_at)].set(least).at[tuple(next_to)].set(largest)


def steps_of(key, shape, cuts, low, high):
    loudness = 1.0
    for position, shards_of in cuts:
        heights = jax.random.uniform(jax.random.fold_in(jax.random.fold_in(key, 6), position), (shards_of,), jnp.float32, low / len(cuts), high / len(cuts))
        loudness = loudness * jnp.repeat(jnp.exp(heights), shape[position] // shards_of).reshape((-1,) + (1,) * (len(shape) - 1 - position))
    return loudness


def gaussian(rng, shape, spread, reach, split=(), held_as=jnp.bfloat16):
    result = spread * jax.random.normal(rng, shape, jnp.float32)
    if split:
        result = result * steps_of(rng, shape, split, -0.22, 0.18)
    return jnp.clip(result, -reach, reach).astype(held_as)


def setup_inputs(seed: int = 0) -> dict:
    arg_keys = jax.random.split(jax.random.key(seed), 9)
    return {
        "cell_index": set_ends(jax.random.randint(arg_keys[0], (2, BUNCHES, 2, PARTS_SIZE), 0, GRID), jax.random.fold_in(arg_keys[0], 1), 0, GRID - 1).astype(jnp.int32),
        "charges": jnp.clip(jnp.exp(math.log(2.0) - 1.3862944 * jax.random.uniform(arg_keys[1], (2, BUNCHES, PARTS_SIZE), jnp.float32) ** steps_of(arg_keys[1], (2, BUNCHES, PARTS_SIZE), ((1, 32), (2, 16)), -0.2, 0.2)), 0.5, 2.0).astype(jnp.bfloat16),
        "momenta": gaussian(arg_keys[2], (2, BUNCHES, 2, PARTS_SIZE), 1.0, 6.0, ((1, 32), (3, 16)), jnp.float32),
        "fill_pattern": set_ends((jax.random.randint(arg_keys[3], (2, BUNCHES), 0, 4) < 3).astype(jnp.int32), jax.random.fold_in(arg_keys[3], 1), 0, 1),
        "encounters": set_ends((jax.random.randint(arg_keys[4], (STOPS, 2, 2, BUNCHES), 0, 2) < 1).astype(jnp.int32), jax.random.fold_in(arg_keys[4], 1), 0, 1),
        "green_spectrum": jnp.clip(jnp.exp(math.log(4.0) - 2.0794415 * jax.random.uniform(arg_keys[5], (GRID, GRID), jnp.float32) ** steps_of(arg_keys[5], (GRID, GRID), ((1, 16),), -0.2, 0.2)), 0.5, 4.0),
        "stop_gain": jnp.clip(jnp.exp(jax.random.uniform(arg_keys[6], (STOPS,), jnp.float32, math.log(0.5), math.log(2.0))), 0.5, 2.0),
        "parasitic_gain": jnp.clip(jnp.exp(jax.random.uniform(arg_keys[7], (STOPS,), jnp.float32, math.log(0.25), math.log(1.0))), 0.25, 1.0),
    }


def shifted_up(operand, amount):
    kept = operand[..., :GRID - amount]
    widths = [(0, 0)] * (operand.ndim - 1) + [(amount, 0)]
    return jnp.pad(kept, widths)


def shifted_down(operand, amount):
    kept = operand[..., amount:]
    widths = [(0, 0)] * (operand.ndim - 1) + [(0, amount)]
    return jnp.pad(kept, widths)


def reference(cell_index, charges, momenta, fill_pattern, encounters, green_spectrum, stop_gain, parasitic_gain):
    flat_cells = cell_index.reshape(2 * BUNCHES, 2, PARTS_SIZE)
    flat_charges = charges.reshape(2 * BUNCHES, PARTS_SIZE)
    flat_fill = fill_pattern.reshape(2 * BUNCHES)

    def one_bunch(operands):
        cells_b, charge_b, fill_b = operands
        density = jnp.zeros((GRID, GRID), jnp.float32).at[cells_b[0], cells_b[1]].add(charge_b.astype(jnp.float32))
        density = density * fill_b.astype(jnp.float32)
        spectrum = jnp.fft.fft2(density)
        potential = jnp.real(jnp.fft.ifft2(green_spectrum * spectrum)).astype(density.dtype)
        along_x = -0.5 * (jnp.roll(potential, -1, 0) - jnp.roll(potential, 1, 0))
        along_y = -0.5 * (jnp.roll(potential, -1, 1) - jnp.roll(potential, 1, 1))
        return jnp.stack([along_x, along_y]).astype(jnp.bfloat16)

    fields = lax.map(one_bunch, (flat_cells, flat_charges, flat_fill)).reshape(2, BUNCHES, 2, GRID, GRID)
    outputs = []
    for beam_index in range(2):
        opposing = fields[1 - beam_index]
        direction = 1 if beam_index == 0 else -1
        partners = [jnp.roll(opposing, -direction * offset * BUN_DEV, axis=0) for offset in range(STOPS + 1)]
        summed = jnp.zeros((BUNCHES, 2, GRID, GRID), jnp.float32)
        for stop_number in range(STOPS):
            summed = summed + stop_gain[stop_number] * partners[stop_number].astype(jnp.float32)
            weight = stop_gain[stop_number] * parasitic_gain[stop_number]
            mark_up = encounters[stop_number, beam_index, 0].astype(jnp.float32)[:, None, None, None]
            following = shifted_up(partners[stop_number + 1].astype(jnp.float32), OFFSET_CELLS)
            summed = summed + weight * mark_up * following
            if stop_number >= 1:
                mark_down = encounters[stop_number, beam_index, 1].astype(jnp.float32)[:, None, None, None]
                earlier = shifted_down(partners[stop_number - 1].astype(jnp.float32), OFFSET_CELLS)
                summed = summed + weight * mark_down * earlier
        total_field = summed.astype(jnp.bfloat16)

        def kick_one(operands):
            field_b, cells_b = operands
            return field_b[:, cells_b[0], cells_b[1]].astype(jnp.float32)

        kick_sum = lax.map(kick_one, (total_field, cell_index[beam_index]))
        outputs.append(momenta[beam_index] + kick_sum)
    return jnp.stack(outputs)
```

```python
import functools
import math

import jax
import jax.numpy as jnp
import ml_dtypes
import numpy as np
from jax import lax
from jax.experimental import pallas as pl
from jax.experimental.pallas import tpu as pltpu
from jax.sharding import PartitionSpec as P

GRID = 256
HALF = GRID // 2
STOPS = 4
OFFSET_CELLS = 32
CHIPS = 8
SLAB = GRID // CHIPS
PAIR = SLAB // 2
CHUNK = 256
MESH = pl.DeviceIdType.MESH
F32 = jnp.float32
BF16 = jnp.bfloat16
RING_ORDER = (4, 3, 5, 2, 6, 1, 7)


def split_np(table):
    high = table.astype(ml_dtypes.bfloat16)
    low = (table - high.astype(np.float64)).astype(ml_dtypes.bfloat16)
    return high, low


def basis_rows(wave, is_sine):
    positions = np.arange(GRID)
    if is_sine and wave == 0:
        return np.cos(math.pi * positions) / 16.0
    if wave == 0:
        return np.full(GRID, 1.0 / 16.0)
    angle = 2.0 * math.pi / GRID * ((wave * positions) % GRID)
    return (np.sin(angle) if is_sine else np.cos(angle)) * math.sqrt(2.0) / 16.0


def fold_row(wave, is_sine):
    row = np.zeros(GRID)
    if wave == 0:
        row[HALF if is_sine else 0] = 1.0
    else:
        row[wave] = 0.5
        row[GRID - wave] = -0.5 if is_sine else 0.5
    return row


def make_tables():
    slab_order = [
        (PAIR * chip + r % PAIR, r >= PAIR) for chip in range(CHIPS) for r in range(SLAB)
    ]
    plain_order = [(q % HALF, q >= HALF) for q in range(GRID)]
    row_basis = np.stack([basis_rows(*entry) for entry in slab_order])
    col_basis = np.stack([basis_rows(*entry) for entry in plain_order])
    row_fold = np.stack([fold_row(*entry) for entry in slab_order])
    col_fold = np.stack([fold_row(*entry) for entry in plain_order]).T
    stacked = np.stack(
        [
            *split_np(row_basis),
            *split_np(col_basis.T),
            *split_np(col_basis),
            row_fold.astype(ml_dtypes.bfloat16),
            col_fold.astype(ml_dtypes.bfloat16),
        ]
    )
    sines = np.sin(2.0 * math.pi / GRID * np.arange(HALF))
    return stacked, np.repeat(sines[:, None], 128, axis=1).astype(np.float32)


def split(value):
    high = value.astype(BF16)
    return high, (value - high.astype(F32)).astype(BF16)


def mm(a, b):
    return jnp.dot(a, b, preferred_element_type=F32)


def mm_nt(a, b):
    return lax.dot_general(a, b, (((1,), (1,)), ((), ())), preferred_element_type=F32)


def mm3(a, b):
    return mm(a[0], b[0]) + (mm(a[0], b[1]) + mm(a[1], b[0]))


def kernel(
    bunches,
    cell_ref,
    charge_ref,
    momenta_ref,
    fill_ref,
    mark_ref,
    green_ref,
    stop_ref,
    para_ref,
    table_ref,
    sine_ref,
    out_ref,
    cells,
    charge,
    charge_other,
    momenta,
    fill,
    marks,
    green,
    stop,
    para,
    table,
    sines,
    wide,
    pack_mine,
    pack_other,
    pack_out,
    pack_in,
    row_hot,
    col_hot,
    row_wave,
    row_wave_low,
    rows_out,
    rows_in,
    spec_out,
    spec_in,
    total,
    kick_out,
    kick_in,
    load_sem,
    swap_send,
    swap_recv,
    pack_send,
    pack_recv,
    rows_send,
    rows_recv,
    spec_send,
    spec_recv,
    total_send,
    total_recv,
    kick_send,
    kick_recv,
):
    parts = cells.shape[2]
    bunch = lax.axis_index("bunch")
    tile = lax.axis_index("tile")
    chip = lax.div(tile, 2)
    core = lax.rem(tile, 2)
    other = 1 - core
    sibling = (bunch, 2 * chip + other)

    def ring(step):
        there = lax.rem(chip + step, CHIPS)
        return there, (bunch, 2 * there + core)

    def meets(step):
        return (lax.rem(bunch + (1 - 2 * core) * step + 4 * bunches, bunches), 2 * chip + other)

    barrier = pltpu.get_barrier_semaphore()
    partners = [meets(step) for step in range(STOPS + 1)] + [ring(step)[1] for step in range(1, CHIPS)]
    for partner in partners:
        pl.semaphore_signal(barrier, inc=1, device_id=partner, device_id_type=MESH)

    loads = [
        pltpu.make_async_copy(source, target, load_sem.at[index])
        for index, (source, target) in enumerate(
            [
                (green_ref, green),
                (table_ref, table),
                (cell_ref.at[core, 0], cells.at[0]),
                (charge_ref, charge),
                (fill_ref, fill),
                (mark_ref, marks),
                (stop_ref, stop),
                (para_ref, para),
                (sine_ref, sines),
                (momenta_ref, momenta),
            ]
        )
    ]
    for load in loads:
        load.start()

    row_basis = (table.at[0], table.at[1])
    to_cols = (table.at[2], table.at[3])
    from_cols = (table.at[4], table.at[5])

    loads[0].wait()
    loads[1].wait()
    wide[...] = jnp.zeros(wide.shape, F32)
    wide[0 : green.shape[0]] = green[...]
    green_high, green_low = split(wide[...])
    folded = mm_nt(table[6], green_high) + mm_nt(table[6], green_low)
    folded = folded.reshape(CHIPS, 4, 8, 128)
    packed = folded[:, 0].reshape(CHIPS * 8, 128)
    for group in range(1, 4):
        packed = packed + pltpu.roll(folded[:, group].reshape(CHIPS * 8, 128), 32 * group, 1)
    packed = pltpu.roll(packed, 16 * core, 1)
    pack_mine[...] = packed.reshape(CHIPS, 8, 128)

    pl.semaphore_wait(barrier, len(partners))

    swaps = [
        pltpu.make_async_remote_copy(
            src_ref=source,
            dst_ref=target,
            send_sem=swap_send.at[index],
            recv_sem=swap_recv.at[index],
            device_id=sibling,
            device_id_type=MESH,
        )
        for index, (source, target) in enumerate(
            [
                (cell_ref.at[other, 0], cells.at[1]),
                (charge_ref, charge_other),
                (pack_mine, pack_other),
            ]
        )
    ]
    for swap in swaps:
        swap.start()

    cell_iota = lax.broadcasted_iota(jnp.int32, (GRID, CHUNK), 0)

    def deposit(half):
        filled = fill[core].astype(F32)
        for first in range(0, parts, CHUNK):
            here = pl.ds(half * parts + first, CHUNK)
            rows = cells[half, 0:1, first : first + CHUNK]
            cols = cells[half, 1:2, first : first + CHUNK]
            both = (charge, charge_other)[half][:, first : first + CHUNK].astype(F32)
            weight = jnp.where(core == 0, both[0:1], both[1:2]) * filled
            row_hot[:, here] = jnp.where(cell_iota == rows, 1.0, 0.0).astype(BF16)
            col_hot[:, here] = jnp.where(cell_iota == cols, weight, 0.0).astype(BF16)
        span = pl.ds(half * parts, parts)
        return mm_nt(row_hot[:, span], col_hot[:, span])

    for load in loads[2:]:
        load.wait()
    density = deposit(0)
    for swap in swaps:
        swap.wait()

    pack_out[...] = pack_mine[...] + pack_other[...]
    pack_in[chip] = pack_out[chip]
    packs = []
    for step in RING_ORDER:
        there, device = ring(step)
        copy = pltpu.make_async_remote_copy(
            src_ref=pack_out.at[there],
            dst_ref=pack_in.at[chip],
            send_sem=pack_send.at[step],
            recv_sem=pack_recv.at[step],
            device_id=device,
            device_id_type=MESH,
        )
        copy.start()
        packs.append(copy)

    density = density + deposit(1)
    basis_high, basis_low = row_basis[0][...], row_basis[1][...]
    partial = mm3((basis_high, basis_low), split(density))
    rows_out[...] = partial.astype(BF16)
    top = partial[0:16]
    first_row = lax.broadcasted_iota(jnp.int32, top.shape, 0) == 0
    rows_out[0:16, :] = jnp.where(first_row, top - jnp.mean(top, axis=1, keepdims=True), top).astype(BF16)
    sums = []
    for step in RING_ORDER:
        there, device = ring(step)
        copy = pltpu.make_async_remote_copy(
            src_ref=rows_out.at[pl.ds(pl.multiple_of(SLAB * there, SLAB), SLAB)],
            dst_ref=rows_in.at[step],
            send_sem=rows_send.at[step],
            recv_sem=rows_recv.at[step],
            device_id=device,
            device_id_type=MESH,
        )
        copy.start()
        sums.append(copy)

    row_wave[...] = mm(basis_high, row_hot[...]).astype(BF16)
    row_wave_low[...] = mm(basis_low, row_hot[...]).astype(BF16)

    for copy in packs:
        copy.wait()
    lane = lax.broadcasted_iota(jnp.int32, (8, 128), 1)
    halves = []
    for side in range(2):
        groups = []
        for group in range(4):
            merged = jnp.zeros((8, 128), F32)
            for spot in range(4):
                moved = pack_in[4 * side + spot]
                shift = (32 * (spot - group)) % 128
                if shift:
                    moved = pltpu.roll(moved, shift, 1)
                merged = jnp.where(lane // 32 == spot, moved, merged)
            groups.append(merged)
        halves.append(jnp.concatenate(groups, axis=0))
    slab_high, slab_low = split(jnp.concatenate(halves, axis=1))
    factors = mm(slab_high, table[7]) + mm(slab_low, table[7])
    lanes = lax.broadcasted_iota(jnp.int32, (PAIR, HALF), 1)
    subs = lax.broadcasted_iota(jnp.int32, (PAIR, HALF), 0)
    special = jnp.logical_and(subs == 0, chip == 0)
    gain_cc = factors[:PAIR, :HALF]
    gain_cs = jnp.where(lanes == 0, factors[:PAIR, HALF:], gain_cc)
    gain_sc = jnp.where(special, factors[PAIR:, :HALF], gain_cc)
    gain_ss = jnp.where(special, jnp.where(lanes == 0, factors[PAIR:, HALF:], factors[PAIR:, :HALF]), gain_cs)
    mixing = jnp.where(jnp.logical_or(special, lanes == 0), 0.0, factors[PAIR:, HALF:])

    for copy in sums:
        copy.wait()
    slab = rows_out[pl.ds(pl.multiple_of(SLAB * chip, SLAB), SLAB), :].astype(F32)
    for step in range(1, CHIPS):
        slab = slab + rows_in[step].astype(F32)
    spectrum = mm3(split(slab), (to_cols[0][...], to_cols[1][...]))
    part_cc, part_cs = spectrum[:PAIR, :HALF], spectrum[:PAIR, HALF:]
    part_sc, part_ss = spectrum[PAIR:, :HALF], spectrum[PAIR:, HALF:]
    upper = jnp.concatenate(
        [gain_cc * part_cc - mixing * part_ss, gain_cs * part_cs + mixing * part_sc], axis=1
    )
    lower = jnp.concatenate(
        [gain_sc * part_sc + mixing * part_cs, gain_ss * part_ss - mixing * part_cc], axis=1
    )
    spec_out[...] = jnp.concatenate([upper, lower], axis=0).astype(spec_out.dtype)
    spectra = []
    for step in (3, 2, 4, 1, 0):
        copy = pltpu.make_async_remote_copy(
            src_ref=spec_out,
            dst_ref=spec_in.at[step],
            send_sem=spec_send.at[step],
            recv_sem=spec_recv.at[step],
            device_id=meets(step),
            device_id_type=MESH,
        )
        copy.start()
        spectra.append(copy)

    gains = [stop[s] for s in range(STOPS)]
    weights = [stop[s] * para[s] for s in range(STOPS)]
    marks_up = [marks[2 * core, s].astype(F32) for s in range(STOPS)]
    marks_down = [marks[2 * core + 1, s].astype(F32) for s in range(STOPS)]
    for copy in spectra:
        copy.wait()
    direct = jnp.zeros((SLAB, GRID), F32)
    upward = jnp.zeros((SLAB, GRID), F32)
    downward = jnp.zeros((SLAB, GRID), F32)
    for step in range(STOPS + 1):
        partner = spec_in[step].astype(F32)
        if step < STOPS:
            direct = direct + gains[step] * partner
        if step >= 1:
            upward = upward + (weights[step - 1] * marks_up[step - 1]) * partner
        if step + 1 < STOPS:
            downward = downward + (weights[step + 1] * marks_down[step + 1]) * partner
    mixed = mm3(
        split(jnp.concatenate([direct, upward, downward], axis=0)),
        (from_cols[0][...], from_cols[1][...]),
    )
    column = lax.broadcasted_iota(jnp.int32, (SLAB, GRID), 1)

    def encounter(three):
        moved_up = jnp.where(column >= OFFSET_CELLS, pltpu.roll(three[SLAB : 2 * SLAB], OFFSET_CELLS, 1), 0.0)
        moved_down = jnp.where(
            column < GRID - OFFSET_CELLS, pltpu.roll(three[2 * SLAB :], GRID - OFFSET_CELLS, 1), 0.0
        )
        return three[:SLAB] + moved_up + moved_down

    smooth = encounter(mixed)
    sine = sines[pl.ds(pl.multiple_of(PAIR * chip, PAIR), PAIR), :]
    sine = jnp.concatenate([sine, sine], axis=1)
    along_x = jnp.concatenate([-sine * smooth[PAIR:], sine * smooth[:PAIR]], axis=0)
    along_y = encounter(-0.5 * (pltpu.roll(mixed, GRID - 1, 1) - pltpu.roll(mixed, 1, 1)))
    mine = pl.ds(pl.multiple_of(SLAB * chip, SLAB), SLAB)
    total[mine, :] = jnp.concatenate([along_x, along_y], axis=1).astype(BF16)
    gathers = []
    for step in RING_ORDER:
        there, device = ring(step)
        copy = pltpu.make_async_remote_copy(
            src_ref=total.at[mine],
            dst_ref=total.at[mine],
            send_sem=total_send.at[step],
            recv_sem=total_recv.at[step],
            device_id=device,
            device_id_type=MESH,
        )
        copy.start()
        gathers.append(copy)
    for copy in gathers:
        copy.wait()

    turned = jnp.transpose(total[...].astype(F32)).astype(BF16)

    def kicks(half, target):
        for first in range(0, parts, CHUNK):
            here = pl.ds(half * parts + first, CHUNK)
            values = mm(turned, row_wave[:, here]) + mm(turned, row_wave_low[:, here])
            hit = cell_iota == cells[half, 1:2, first : first + CHUNK]
            for axis in range(2):
                picked = jnp.where(hit, values[axis * GRID : (axis + 1) * GRID], 0.0)
                target(axis, first, jnp.sum(picked, axis=0, keepdims=True))

    def to_sibling(axis, first, value):
        kick_out[axis : axis + 1, first : first + CHUNK] = value

    def to_output(axis, first, value):
        out_ref[core, 0, axis : axis + 1, first : first + CHUNK] = (
            momenta[core, 0, axis : axis + 1, first : first + CHUNK] + value
        )

    kicks(1, to_sibling)
    back = pltpu.make_async_remote_copy(
        src_ref=kick_out,
        dst_ref=kick_in,
        send_sem=kick_send,
        recv_sem=kick_recv,
        device_id=sibling,
        device_id_type=MESH,
    )
    back.start()
    kicks(0, to_output)
    back.wait()
    out_ref[other, 0] = momenta[other, 0] + kick_in[...]


def body(bunches, tables, *operands):
    cell_index, charges, momenta, fill_pattern, encounters, green_spectrum, stop_gain, parasitic_gain = operands
    parts = cell_index.shape[3]
    stacked, sines = tables
    charges = charges.reshape(2, parts)
    fill_pattern = fill_pattern.reshape(2)
    encounters = encounters.reshape(STOPS, 2, 2).transpose(1, 2, 0).reshape(4, STOPS)
    green_spectrum = green_spectrum.T
    operands = (cell_index, charges, momenta, fill_pattern, encounters, green_spectrum, stop_gain, parasitic_gain)
    any_spec = pl.BlockSpec(memory_space=pltpu.HBM)
    dma = pltpu.SemaphoreType.DMA
    return pl.pallas_call(
        functools.partial(kernel, bunches),
        out_shape=jax.ShapeDtypeStruct(momenta.shape, F32),
        in_specs=[any_spec] * 10,
        out_specs=pl.BlockSpec(memory_space=pltpu.VMEM),
        scratch_shapes=[
            pltpu.VMEM((2, 2, parts), jnp.int32),
            pltpu.VMEM((2, parts), BF16),
            pltpu.VMEM((2, parts), BF16),
            pltpu.VMEM((2, 1, 2, parts), F32),
            pltpu.SMEM(fill_pattern.shape, jnp.int32),
            pltpu.SMEM(encounters.shape, jnp.int32),
            pltpu.VMEM(green_spectrum.shape, F32),
            pltpu.SMEM(stop_gain.shape, F32),
            pltpu.SMEM(parasitic_gain.shape, F32),
            pltpu.VMEM(stacked.shape, BF16),
            pltpu.VMEM(sines.shape, F32),
            pltpu.VMEM((128, GRID), F32),
            pltpu.VMEM((CHIPS, 8, 128), F32),
            pltpu.VMEM((CHIPS, 8, 128), F32),
            pltpu.VMEM((CHIPS, 8, 128), F32),
            pltpu.VMEM((CHIPS, 8, 128), F32),
            pltpu.VMEM((GRID, 2 * parts), BF16),
            pltpu.VMEM((GRID, 2 * parts), BF16),
            pltpu.VMEM((GRID, 2 * parts), BF16),
            pltpu.VMEM((GRID, 2 * parts), BF16),
            pltpu.VMEM((GRID, GRID), BF16),
            pltpu.VMEM((CHIPS, SLAB, GRID), BF16),
            pltpu.VMEM((SLAB, GRID), F32),
            pltpu.VMEM((STOPS + 1, SLAB, GRID), F32),
            pltpu.VMEM((GRID, 2 * GRID), BF16),
            pltpu.VMEM((2, parts), F32),
            pltpu.VMEM((2, parts), F32),
            dma((10,)),
            dma((3,)),
            dma((3,)),
            dma((CHIPS,)),
            dma((CHIPS,)),
            dma((CHIPS,)),
            dma((CHIPS,)),
            dma((STOPS + 1,)),
            dma((STOPS + 1,)),
            dma((CHIPS,)),
            dma((CHIPS,)),
            dma(()),
            dma(()),
        ],
        compiler_params=pltpu.CompilerParams(
            collective_id=0, has_side_effects=True, vmem_limit_bytes=60 << 20
        ),
    )(*operands, stacked, sines)


def solution(mesh):
    in_specs = (
        P(None, "bunch", None, "tile"),
        P(None, "bunch", "tile"),
        P(None, "bunch", None, "tile"),
        P(None, "bunch"),
        P(None, None, None, "bunch"),
        P(None, "tile"),
        P(),
        P(),
    )
    out_specs = P(None, "bunch", None, "tile")
    tables = make_tables()
    return jax.shard_map(
        functools.partial(body, mesh.shape["bunch"], tables),
        mesh=mesh,
        in_specs=in_specs,
        out_specs=out_specs,
        check_vma=False,
    )
```

```python
import functools
import math

import jax
import jax.numpy as jnp
import ml_dtypes
import numpy as np
from jax import lax
from jax.experimental import pallas as pl
from jax.experimental.pallas import tpu as pltpu
from jax.sharding import PartitionSpec as P

GRID = 256
HALF = GRID // 2
STOPS = 4
OFFSET_CELLS = 32
CHIPS = 8
SLAB = GRID // CHIPS
HALVES = 2
PART = SLAB // HALVES
PAIR = PART // 2
CHUNK = 256
LEAD = 4
MESH = pl.DeviceIdType.MESH
F32 = jnp.float32
BF16 = jnp.bfloat16
RING_ORDER = (4, 3, 5, 2, 6, 1, 7)


def split_np(table):
    high = table.astype(ml_dtypes.bfloat16)
    low = (table - high.astype(np.float64)).astype(ml_dtypes.bfloat16)
    return high, low


def basis_rows(wave, is_sine):
    positions = np.arange(GRID)
    if is_sine and wave == 0:
        return np.cos(math.pi * positions) / 16.0
    if wave == 0:
        return np.full(GRID, 1.0 / 16.0)
    angle = 2.0 * math.pi / GRID * ((wave * positions) % GRID)
    return (np.sin(angle) if is_sine else np.cos(angle)) * math.sqrt(2.0) / 16.0


def fold_row(wave, is_sine):
    row = np.zeros(GRID)
    if wave == 0:
        row[HALF if is_sine else 0] = 1.0
    else:
        row[wave] = 0.5
        row[GRID - wave] = -0.5 if is_sine else 0.5
    return row


def make_tables():
    slab_order = [
        (PAIR * part + r % PAIR, r >= PAIR) for part in range(CHIPS * HALVES) for r in range(PART)
    ]
    plain_order = [(q % HALF, q >= HALF) for q in range(GRID)]
    row_basis = np.stack([basis_rows(*entry) for entry in slab_order])
    col_basis = np.stack([basis_rows(*entry) for entry in plain_order])
    row_fold = np.stack([fold_row(*entry) for entry in slab_order])
    col_fold = np.stack([fold_row(*entry) for entry in plain_order]).T
    stacked = np.stack(
        [
            *split_np(row_basis),
            *split_np(col_basis.T),
            *split_np(col_basis),
            row_fold.astype(ml_dtypes.bfloat16),
            col_fold.astype(ml_dtypes.bfloat16),
        ]
    )
    sines = np.sin(2.0 * math.pi / GRID * np.arange(HALF))
    return stacked, np.repeat(sines[:, None], 128, axis=1).astype(np.float32)


def split(value):
    high = value.astype(BF16)
    return high, (value - high.astype(F32)).astype(BF16)


def mm(a, b):
    return jnp.dot(a, b, preferred_element_type=F32)


def mm_nt(a, b):
    return lax.dot_general(a, b, (((1,), (1,)), ((), ())), preferred_element_type=F32)


def mm3(a, b):
    return mm(a[0], b[0]) + (mm(a[0], b[1]) + mm(a[1], b[0]))


def kernel(
    bunches,
    cell_ref,
    charge_ref,
    momenta_ref,
    fill_ref,
    mark_ref,
    green_ref,
    stop_ref,
    para_ref,
    table_ref,
    sine_ref,
    out_ref,
    cells,
    charge,
    charge_other,
    momenta,
    fill,
    marks,
    green,
    stop,
    para,
    table,
    sines,
    wide,
    pack_mine,
    pack_other,
    pack_out,
    pack_in,
    row_hot,
    col_hot,
    row_wave,
    row_wave_low,
    rows_out,
    rows_in,
    spec_out,
    spec_in,
    total,
    kick_out,
    kick_in,
    load_sem,
    swap_send,
    swap_recv,
    pack_send,
    pack_recv,
    rows_send,
    rows_recv,
    spec_send,
    spec_recv,
    total_send,
    total_recv,
    kick_send,
    kick_recv,
    ring_in,
    met_in,
):
    parts = cells.shape[2]
    bunch = lax.axis_index("bunch")
    tile = lax.axis_index("tile")
    chip = lax.div(tile, 2)
    core = lax.rem(tile, 2)
    other = 1 - core
    sibling = (bunch, 2 * chip + other)

    def ring(step):
        there = lax.rem(chip + step, CHIPS)
        return there, (bunch, 2 * there + core)

    def meets(step):
        return (lax.rem(bunch + (1 - 2 * core) * step + 4 * bunches, bunches), 2 * chip + other)

    barrier = pltpu.get_barrier_semaphore()
    leads = lax.rem(chip, LEAD) == 0
    near = [sibling] + [ring(step)[1] for step in range(1, CHIPS)]
    for partner in near:
        pl.semaphore_signal(barrier, inc=1, device_id=partner, device_id_type=MESH)

    @pl.when(leads)
    def _():
        for step in range(1, STOPS + 1):
            pl.semaphore_signal(barrier, inc=1, device_id=meets(step), device_id_type=MESH)

    loads = [
        pltpu.make_async_copy(source, target, load_sem.at[index])
        for index, (source, target) in enumerate(
            [
                (green_ref, green),
                (table_ref, table),
                (cell_ref.at[core, 0], cells.at[0]),
                (charge_ref, charge),
                (fill_ref, fill),
                (mark_ref, marks),
                (stop_ref, stop),
                (para_ref, para),
                (sine_ref, sines),
                (momenta_ref, momenta),
            ]
        )
    ]
    for load in loads:
        load.start()

    row_basis = (table.at[0], table.at[1])
    to_cols = (table.at[2], table.at[3])
    from_cols = (table.at[4], table.at[5])

    loads[0].wait()
    loads[1].wait()
    wide[...] = jnp.zeros(wide.shape, F32)
    wide[0 : green.shape[0]] = green[...]
    green_high, green_low = split(wide[...])
    folded = mm_nt(table[6], green_high) + mm_nt(table[6], green_low)
    folded = folded.reshape(CHIPS, 4, 8, 128)
    packed = folded[:, 0].reshape(CHIPS * 8, 128)
    for group in range(1, 4):
        packed = packed + pltpu.roll(folded[:, group].reshape(CHIPS * 8, 128), 32 * group, 1)
    packed = pltpu.roll(packed, 16 * core, 1)
    pack_mine[...] = packed.reshape(CHIPS, 8, 128)

    pl.semaphore_wait(barrier, jnp.where(leads, len(near) + STOPS, len(near)))

    @pl.when(leads)
    def _():
        for step in range(1, STOPS + 1):
            pl.semaphore_signal(ring_in, inc=1, device_id=meets(step), device_id_type=MESH)

    swaps = [
        pltpu.make_async_remote_copy(
            src_ref=source,
            dst_ref=target,
            send_sem=swap_send.at[index],
            recv_sem=swap_recv.at[index],
            device_id=sibling,
            device_id_type=MESH,
        )
        for index, (source, target) in enumerate(
            [
                (cell_ref.at[other, 0], cells.at[1]),
                (charge_ref, charge_other),
                (pack_mine, pack_other),
            ]
        )
    ]
    for swap in swaps:
        swap.start()

    cell_iota = lax.broadcasted_iota(jnp.int32, (GRID, CHUNK), 0)

    def deposit(half):
        filled = fill[core].astype(F32)
        for first in range(0, parts, CHUNK):
            here = pl.ds(half * parts + first, CHUNK)
            rows = cells[half, 0:1, first : first + CHUNK]
            cols = cells[half, 1:2, first : first + CHUNK]
            both = (charge, charge_other)[half][:, first : first + CHUNK].astype(F32)
            weight = jnp.where(core == 0, both[0:1], both[1:2]) * filled
            row_hot[:, here] = jnp.where(cell_iota == rows, 1.0, 0.0).astype(BF16)
            col_hot[:, here] = jnp.where(cell_iota == cols, weight, 0.0).astype(BF16)
        span = pl.ds(half * parts, parts)
        return mm_nt(row_hot[:, span], col_hot[:, span])

    for load in loads[2:]:
        load.wait()
    density = deposit(0)
    for swap in swaps:
        swap.wait()

    pack_out[...] = pack_mine[...] + pack_other[...]
    pack_in[chip] = pack_out[chip]
    packs = []
    for step in RING_ORDER:
        there, device = ring(step)
        copy = pltpu.make_async_remote_copy(
            src_ref=pack_out.at[there],
            dst_ref=pack_in.at[chip],
            send_sem=pack_send.at[step],
            recv_sem=pack_recv.at[step],
            device_id=device,
            device_id_type=MESH,
        )
        copy.start()
        packs.append(copy)

    density = density + deposit(1)
    basis_high, basis_low = row_basis[0][...], row_basis[1][...]
    partial = mm3((basis_high, basis_low), split(density))
    rows_out[...] = partial.astype(BF16)
    top = partial[0:16]
    first_row = lax.broadcasted_iota(jnp.int32, top.shape, 0) == 0
    rows_out[0:16, :] = jnp.where(first_row, top - jnp.mean(top, axis=1, keepdims=True), top).astype(BF16)
    sums = [[] for _ in range(HALVES)]
    for part in range(HALVES):
        for step in RING_ORDER:
            there, device = ring(step)
            first = pl.multiple_of(SLAB * there + PART * part, PART)
            copy = pltpu.make_async_remote_copy(
                src_ref=rows_out.at[pl.ds(first, PART)],
                dst_ref=rows_in.at[part, step],
                send_sem=rows_send.at[part, step],
                recv_sem=rows_recv.at[part, step],
                device_id=device,
                device_id_type=MESH,
            )
            copy.start()
            sums[part].append(copy)

    row_wave[...] = mm(basis_high, row_hot[...]).astype(BF16)
    row_wave_low[...] = mm(basis_low, row_hot[...]).astype(BF16)

    @pl.when(leads)
    def _():
        pl.semaphore_wait(ring_in, STOPS)
        for ahead in range(1, LEAD):
            follower = (bunch, 2 * (chip + ahead) + core)
            pl.semaphore_signal(met_in, inc=1, device_id=follower, device_id_type=MESH)

    for copy in packs:
        copy.wait()
    lane = lax.broadcasted_iota(jnp.int32, (8, 128), 1)
    halves = []
    for side in range(2):
        groups = []
        for group in range(4):
            merged = jnp.zeros((8, 128), F32)
            for spot in range(4):
                moved = pack_in[4 * side + spot]
                shift = (32 * (spot - group)) % 128
                if shift:
                    moved = pltpu.roll(moved, shift, 1)
                merged = jnp.where(lane // 32 == spot, moved, merged)
            groups.append(merged)
        halves.append(jnp.concatenate(groups, axis=0))
    slab_high, slab_low = split(jnp.concatenate(halves, axis=1))
    factors = mm(slab_high, table[7]) + mm(slab_low, table[7])
    lanes = lax.broadcasted_iota(jnp.int32, (PAIR, HALF), 1)
    subs = lax.broadcasted_iota(jnp.int32, (PAIR, HALF), 0)

    def convolve(part):
        even = factors[PART * part : PART * part + PAIR]
        odd = factors[PART * part + PAIR : PART * (part + 1)]
        gain_cc = even[:, :HALF]
        gain_cs = jnp.where(lanes == 0, even[:, HALF:], gain_cc)
        gain_sc, gain_ss, edge = gain_cc, gain_cs, lanes == 0
        if part == 0:
            special = jnp.logical_and(subs == 0, chip == 0)
            gain_sc = jnp.where(special, odd[:, :HALF], gain_cc)
            gain_ss = jnp.where(special, jnp.where(lanes == 0, odd[:, HALF:], odd[:, :HALF]), gain_cs)
            edge = jnp.logical_or(special, lanes == 0)
        mixing = jnp.where(edge, 0.0, odd[:, HALF:])
        slab = rows_out[pl.ds(pl.multiple_of(SLAB * chip + PART * part, PART), PART), :].astype(F32)
        for step in range(1, CHIPS):
            slab = slab + rows_in[part, step].astype(F32)
        spectrum = mm3(split(slab), (to_cols[0][...], to_cols[1][...]))
        part_cc, part_cs = spectrum[:PAIR, :HALF], spectrum[:PAIR, HALF:]
        part_sc, part_ss = spectrum[PAIR:, :HALF], spectrum[PAIR:, HALF:]
        spec_out[part, :PAIR, :HALF] = gain_cc * part_cc - mixing * part_ss
        spec_out[part, :PAIR, HALF:] = gain_cs * part_cs + mixing * part_sc
        spec_out[part, PAIR:, :HALF] = gain_sc * part_sc + mixing * part_cs
        spec_out[part, PAIR:, HALF:] = gain_ss * part_ss - mixing * part_cc

    spectra = [[] for _ in range(HALVES)]
    for part in range(HALVES):
        for copy in sums[part]:
            copy.wait()
        convolve(part)
        if part == 0:

            @pl.when(jnp.logical_not(leads))
            def _():
                pl.semaphore_wait(met_in, 1)

        for step in (3, 2, 4, 1, 0):
            copy = pltpu.make_async_remote_copy(
                src_ref=spec_out.at[part],
                dst_ref=spec_in.at[part, step],
                send_sem=spec_send.at[part, step],
                recv_sem=spec_recv.at[part, step],
                device_id=meets(step),
                device_id_type=MESH,
            )
            copy.start()
            spectra[part].append(copy)

    gains = [stop[s] for s in range(STOPS)]
    weights = [stop[s] * para[s] for s in range(STOPS)]
    marks_up = [marks[2 * core, s].astype(F32) for s in range(STOPS)]
    marks_down = [marks[2 * core + 1, s].astype(F32) for s in range(STOPS)]
    column = lax.broadcasted_iota(jnp.int32, (PART, GRID), 1)

    def encounter(three):
        moved_up = jnp.where(column >= OFFSET_CELLS, pltpu.roll(three[PART : 2 * PART], OFFSET_CELLS, 1), 0.0)
        moved_down = jnp.where(
            column < GRID - OFFSET_CELLS, pltpu.roll(three[2 * PART :], GRID - OFFSET_CELLS, 1), 0.0
        )
        return three[:PART] + moved_up + moved_down

    def collect(part):
        direct = jnp.zeros((PART, GRID), F32)
        upward = jnp.zeros((PART, GRID), F32)
        downward = jnp.zeros((PART, GRID), F32)
        for step in range(STOPS + 1):
            partner = spec_in[part, step]
            if step < STOPS:
                direct = direct + gains[step] * partner
            if step >= 1:
                upward = upward + (weights[step - 1] * marks_up[step - 1]) * partner
            if step + 1 < STOPS:
                downward = downward + (weights[step + 1] * marks_down[step + 1]) * partner
        mixed = mm3(
            split(jnp.concatenate([direct, upward, downward], axis=0)),
            (from_cols[0][...], from_cols[1][...]),
        )
        smooth = encounter(mixed)
        sine = sines[pl.ds(pl.multiple_of(PAIR * (HALVES * chip + part), PAIR), PAIR), :]
        sine = jnp.concatenate([sine, sine], axis=1)
        along_x = jnp.concatenate([-sine * smooth[PAIR:], sine * smooth[:PAIR]], axis=0)
        along_y = encounter(-0.5 * (pltpu.roll(mixed, GRID - 1, 1) - pltpu.roll(mixed, 1, 1)))
        return jnp.concatenate([along_x, along_y], axis=1).astype(BF16)

    gathers = []
    for part in range(HALVES):
        for copy in spectra[part]:
            copy.wait()
        mine = pl.ds(pl.multiple_of(SLAB * chip + PART * part, PART), PART)
        total[mine, :] = collect(part)
        for step in RING_ORDER:
            there, device = ring(step)
            copy = pltpu.make_async_remote_copy(
                src_ref=total.at[mine],
                dst_ref=total.at[mine],
                send_sem=total_send.at[part, step],
                recv_sem=total_recv.at[part, step],
                device_id=device,
                device_id_type=MESH,
            )
            copy.start()
            gathers.append(copy)
    for copy in gathers:
        copy.wait()

    turned = jnp.transpose(total[...].astype(F32)).astype(BF16)

    def kicks(half, target):
        for first in range(0, parts, CHUNK):
            here = pl.ds(half * parts + first, CHUNK)
            values = mm(turned, row_wave[:, here]) + mm(turned, row_wave_low[:, here])
            hit = cell_iota == cells[half, 1:2, first : first + CHUNK]
            for axis in range(2):
                picked = jnp.where(hit, values[axis * GRID : (axis + 1) * GRID], 0.0)
                target(axis, first, jnp.sum(picked, axis=0, keepdims=True))

    def to_sibling(axis, first, value):
        kick_out[axis : axis + 1, first : first + CHUNK] = value

    def to_output(axis, first, value):
        out_ref[core, 0, axis : axis + 1, first : first + CHUNK] = (
            momenta[core, 0, axis : axis + 1, first : first + CHUNK] + value
        )

    kicks(1, to_sibling)
    back = pltpu.make_async_remote_copy(
        src_ref=kick_out,
        dst_ref=kick_in,
        send_sem=kick_send,
        recv_sem=kick_recv,
        device_id=sibling,
        device_id_type=MESH,
    )
    back.start()
    kicks(0, to_output)
    back.wait()
    out_ref[other, 0] = momenta[other, 0] + kick_in[...]


def body(bunches, tables, *operands):
    cell_index, charges, momenta, fill_pattern, encounters, green_spectrum, stop_gain, parasitic_gain = operands
    parts = cell_index.shape[3]
    stacked, sines = tables
    charges = charges.reshape(2, parts)
    fill_pattern = fill_pattern.reshape(2)
    encounters = encounters.reshape(STOPS, 2, 2).transpose(1, 2, 0).reshape(4, STOPS)
    green_spectrum = green_spectrum.T
    operands = (cell_index, charges, momenta, fill_pattern, encounters, green_spectrum, stop_gain, parasitic_gain)
    any_spec = pl.BlockSpec(memory_space=pltpu.HBM)
    dma = pltpu.SemaphoreType.DMA
    return pl.pallas_call(
        functools.partial(kernel, bunches),
        out_shape=jax.ShapeDtypeStruct(momenta.shape, F32),
        in_specs=[any_spec] * 10,
        out_specs=pl.BlockSpec(memory_space=pltpu.VMEM),
        scratch_shapes=[
            pltpu.VMEM((2, 2, parts), jnp.int32),
            pltpu.VMEM((2, parts), BF16),
            pltpu.VMEM((2, parts), BF16),
            pltpu.VMEM((2, 1, 2, parts), F32),
            pltpu.SMEM(fill_pattern.shape, jnp.int32),
            pltpu.SMEM(encounters.shape, jnp.int32),
            pltpu.VMEM(green_spectrum.shape, F32),
            pltpu.SMEM(stop_gain.shape, F32),
            pltpu.SMEM(parasitic_gain.shape, F32),
            pltpu.VMEM(stacked.shape, BF16),
            pltpu.VMEM(sines.shape, F32),
            pltpu.VMEM((128, GRID), F32),
            pltpu.VMEM((CHIPS, 8, 128), F32),
            pltpu.VMEM((CHIPS, 8, 128), F32),
            pltpu.VMEM((CHIPS, 8, 128), F32),
            pltpu.VMEM((CHIPS, 8, 128), F32),
            pltpu.VMEM((GRID, 2 * parts), BF16),
            pltpu.VMEM((GRID, 2 * parts), BF16),
            pltpu.VMEM((GRID, 2 * parts), BF16),
            pltpu.VMEM((GRID, 2 * parts), BF16),
            pltpu.VMEM((GRID, GRID), BF16),
            pltpu.VMEM((HALVES, CHIPS, PART, GRID), BF16),
            pltpu.VMEM((HALVES, PART, GRID), F32),
            pltpu.VMEM((HALVES, STOPS + 1, PART, GRID), F32),
            pltpu.VMEM((GRID, 2 * GRID), BF16),
            pltpu.VMEM((2, parts), F32),
            pltpu.VMEM((2, parts), F32),
            dma((10,)),
            dma((3,)),
            dma((3,)),
            dma((CHIPS,)),
            dma((CHIPS,)),
            dma((HALVES, CHIPS)),
            dma((HALVES, CHIPS)),
            dma((HALVES, STOPS + 1)),
            dma((HALVES, STOPS + 1)),
            dma((HALVES, CHIPS)),
            dma((HALVES, CHIPS)),
            dma(()),
            dma(()),
            pltpu.SemaphoreType.REGULAR,
            pltpu.SemaphoreType.REGULAR,
        ],
        compiler_params=pltpu.CompilerParams(
            collective_id=0, has_side_effects=True, vmem_limit_bytes=60 << 20
        ),
    )(*operands, stacked, sines)


def solution(mesh):
    in_specs = (
        P(None, "bunch", None, "tile"),
        P(None, "bunch", "tile"),
        P(None, "bunch", None, "tile"),
        P(None, "bunch"),
        P(None, None, None, "bunch"),
        P(None, "tile"),
        P(),
        P(),
    )
    out_specs = P(None, "bunch", None, "tile")
    tables = make_tables()
    return jax.shard_map(
        functools.partial(body, mesh.shape["bunch"], tables),
        mesh=mesh,
        in_specs=in_specs,
        out_specs=out_specs,
        check_vma=False,
    )
```

```python
import functools
import math

import jax
import jax.numpy as jnp
import ml_dtypes
import numpy as np
from jax import lax
from jax.experimental import pallas as pl
from jax.experimental.pallas import tpu as pltpu
from jax.sharding import PartitionSpec as P

GRID = 256
HALF = GRID // 2
STOPS = 4
OFFSET_CELLS = 32
CHIPS = 8
SLAB = GRID // CHIPS
HALVES = 2
PART = SLAB // HALVES
PAIR = PART // 2
CHUNK = 256
LEAD = 4
MESH = pl.DeviceIdType.MESH
F32 = jnp.float32
BF16 = jnp.bfloat16
RING_ORDER = (4, 3, 5, 2, 6, 1, 7)


def split_np(table):
    high = table.astype(ml_dtypes.bfloat16)
    low = (table - high.astype(np.float64)).astype(ml_dtypes.bfloat16)
    return high, low


def basis_rows(wave, is_sine):
    positions = np.arange(GRID)
    if is_sine and wave == 0:
        return np.cos(math.pi * positions) / 16.0
    if wave == 0:
        return np.full(GRID, 1.0 / 16.0)
    angle = 2.0 * math.pi / GRID * ((wave * positions) % GRID)
    return (np.sin(angle) if is_sine else np.cos(angle)) * math.sqrt(2.0) / 16.0


def fold_row(wave, is_sine):
    row = np.zeros(GRID)
    if wave == 0:
        row[HALF if is_sine else 0] = 1.0
    else:
        row[wave] = 0.5
        row[GRID - wave] = -0.5 if is_sine else 0.5
    return row


def make_tables():
    slab_order = [
        (PAIR * part + r % PAIR, r >= PAIR) for part in range(CHIPS * HALVES) for r in range(PART)
    ]
    half_order = [
        slab_order[SLAB * chip + PART * part + r]
        for part in range(HALVES)
        for chip in range(CHIPS)
        for r in range(PART)
    ]
    plain_order = [(q % HALF, q >= HALF) for q in range(GRID)]
    row_basis = np.stack([basis_rows(*entry) for entry in half_order])
    col_basis = np.stack([basis_rows(*entry) for entry in plain_order])
    row_fold = np.stack([fold_row(*entry) for entry in slab_order])
    col_fold = np.stack([fold_row(*entry) for entry in plain_order]).T
    stacked = np.stack(
        [
            *split_np(row_basis),
            *split_np(col_basis.T),
            *split_np(col_basis),
            row_fold.astype(ml_dtypes.bfloat16),
            col_fold.astype(ml_dtypes.bfloat16),
        ]
    )
    sines = np.sin(2.0 * math.pi / GRID * np.arange(HALF))
    return stacked, np.repeat(sines[:, None], 128, axis=1).astype(np.float32)


def split(value):
    high = value.astype(BF16)
    return high, (value - high.astype(F32)).astype(BF16)


def mm(a, b):
    return jnp.dot(a, b, preferred_element_type=F32)


def mm_nt(a, b):
    return lax.dot_general(a, b, (((1,), (1,)), ((), ())), preferred_element_type=F32)


def mm3(a, b):
    return mm(a[0], b[0]) + (mm(a[0], b[1]) + mm(a[1], b[0]))


def kernel(
    bunches,
    cell_ref,
    charge_ref,
    momenta_ref,
    fill_ref,
    mark_ref,
    green_ref,
    stop_ref,
    para_ref,
    table_ref,
    sine_ref,
    out_ref,
    cells,
    charge,
    charge_other,
    momenta,
    fill,
    marks,
    green,
    stop,
    para,
    table,
    sines,
    wide,
    pack_mine,
    pack_other,
    pack_out,
    pack_in,
    row_hot,
    col_hot,
    row_wave,
    kick_first,
    rows_out,
    rows_in,
    spec_out,
    spec_in,
    total,
    kick_out,
    kick_in,
    load_sem,
    swap_send,
    swap_recv,
    pack_send,
    pack_recv,
    rows_send,
    rows_recv,
    spec_send,
    spec_recv,
    total_send,
    total_recv,
    kick_send,
    kick_recv,
    ring_in,
    met_in,
):
    parts = cells.shape[2]
    bunch = lax.axis_index("bunch")
    tile = lax.axis_index("tile")
    chip = lax.div(tile, 2)
    core = lax.rem(tile, 2)
    other = 1 - core
    sibling = (bunch, 2 * chip + other)

    def ring(step):
        there = lax.rem(chip + step, CHIPS)
        return there, (bunch, 2 * there + core)

    def meets(step):
        return (lax.rem(bunch + (1 - 2 * core) * step + 4 * bunches, bunches), 2 * chip + other)

    barrier = pltpu.get_barrier_semaphore()
    leads = lax.rem(chip, LEAD) == 0
    near = [sibling] + [ring(step)[1] for step in range(1, CHIPS)]
    for partner in near:
        pl.semaphore_signal(barrier, inc=1, device_id=partner, device_id_type=MESH)

    @pl.when(leads)
    def _():
        for step in range(1, STOPS + 1):
            pl.semaphore_signal(barrier, inc=1, device_id=meets(step), device_id_type=MESH)

    loads = [
        pltpu.make_async_copy(source, target, load_sem.at[index])
        for index, (source, target) in enumerate(
            [
                (green_ref, green),
                (table_ref, table),
                (cell_ref.at[core, 0], cells.at[0]),
                (charge_ref, charge),
                (fill_ref, fill),
                (mark_ref, marks),
                (stop_ref, stop),
                (para_ref, para),
                (sine_ref, sines),
                (momenta_ref, momenta),
            ]
        )
    ]
    for load in loads:
        load.start()

    row_basis = (table.at[0], table.at[1])
    to_cols = (table.at[2], table.at[3])
    from_cols = (table.at[4], table.at[5])

    loads[0].wait()
    loads[1].wait()
    wide[...] = jnp.zeros(wide.shape, F32)
    wide[0 : green.shape[0]] = green[...]
    green_high, green_low = split(wide[...])
    folded = mm_nt(table[6], green_high) + mm_nt(table[6], green_low)
    folded = folded.reshape(CHIPS, 4, 8, 128)
    packed = folded[:, 0].reshape(CHIPS * 8, 128)
    for group in range(1, 4):
        packed = packed + pltpu.roll(folded[:, group].reshape(CHIPS * 8, 128), 32 * group, 1)
    packed = pltpu.roll(packed, 16 * core, 1)
    pack_mine[...] = packed.reshape(CHIPS, 8, 128)

    pl.semaphore_wait(barrier, jnp.where(leads, len(near) + STOPS, len(near)))

    @pl.when(leads)
    def _():
        for step in range(1, STOPS + 1):
            pl.semaphore_signal(ring_in, inc=1, device_id=meets(step), device_id_type=MESH)

    swaps = [
        pltpu.make_async_remote_copy(
            src_ref=source,
            dst_ref=target,
            send_sem=swap_send.at[index],
            recv_sem=swap_recv.at[index],
            device_id=sibling,
            device_id_type=MESH,
        )
        for index, (source, target) in enumerate(
            [
                (cell_ref.at[other, 0], cells.at[1]),
                (charge_ref, charge_other),
                (pack_mine, pack_other),
            ]
        )
    ]
    for swap in swaps:
        swap.start()

    cell_iota = lax.broadcasted_iota(jnp.int32, (GRID, CHUNK), 0)

    def deposit(half):
        filled = fill[core].astype(F32)
        for first in range(0, parts, CHUNK):
            here = pl.ds(half * parts + first, CHUNK)
            rows = cells[half, 0:1, first : first + CHUNK]
            cols = cells[half, 1:2, first : first + CHUNK]
            both = (charge, charge_other)[half][:, first : first + CHUNK].astype(F32)
            weight = jnp.where(core == 0, both[0:1], both[1:2]) * filled
            row_hot[:, here] = jnp.where(cell_iota == rows, 1.0, 0.0).astype(BF16)
            col_hot[:, here] = jnp.where(cell_iota == cols, weight, 0.0).astype(BF16)
        span = pl.ds(half * parts, parts)
        return mm_nt(row_hot[:, span], col_hot[:, span])

    for load in loads[2:]:
        load.wait()
    density = deposit(0)
    for swap in swaps:
        swap.wait_recv()

    pack_out[...] = pack_mine[...] + pack_other[...]
    pack_in[chip] = pack_out[chip]
    packs = []
    for step in RING_ORDER:
        there, device = ring(step)
        copy = pltpu.make_async_remote_copy(
            src_ref=pack_out.at[there],
            dst_ref=pack_in.at[chip],
            send_sem=pack_send.at[step],
            recv_sem=pack_recv.at[step],
            device_id=device,
            device_id_type=MESH,
        )
        copy.start()
        packs.append(copy)

    density = density + deposit(1)
    basis_high, basis_low = row_basis[0][...], row_basis[1][...]
    pieces = split(density)
    partial = mm3((basis_high[:HALF], basis_low[:HALF]), pieces)
    rows_out[:HALF, :] = partial.astype(BF16)
    top = partial[0:16]
    first_row = lax.broadcasted_iota(jnp.int32, top.shape, 0) == 0
    rows_out[0:16, :] = jnp.where(first_row, top - jnp.mean(top, axis=1, keepdims=True), top).astype(BF16)
    sums = [[] for _ in range(HALVES)]
    for part in range(HALVES):
        if part == 1:
            rows_out[HALF:, :] = mm3((basis_high[HALF:], basis_low[HALF:]), pieces).astype(BF16)
        for step in RING_ORDER:
            there, device = ring(step)
            first = pl.multiple_of(HALF * part + PART * there, PART)
            copy = pltpu.make_async_remote_copy(
                src_ref=rows_out.at[pl.ds(first, PART)],
                dst_ref=rows_in.at[part, step],
                send_sem=rows_send.at[part, step],
                recv_sem=rows_recv.at[part, step],
                device_id=device,
                device_id_type=MESH,
            )
            copy.start()
            sums[part].append(copy)

    for part in range(HALVES):
        span = slice(HALF * part, HALF * (part + 1))
        both = jnp.concatenate([basis_high[span], basis_low[span]], axis=0)
        row_wave[part] = mm(both, row_hot[...]).astype(BF16)

    @pl.when(leads)
    def _():
        pl.semaphore_wait(ring_in, STOPS)
        for ahead in range(1, LEAD):
            follower = (bunch, 2 * (chip + ahead) + core)
            pl.semaphore_signal(met_in, inc=1, device_id=follower, device_id_type=MESH)

    for copy in packs:
        copy.wait_recv()
    lane = lax.broadcasted_iota(jnp.int32, (8, 128), 1)
    halves = []
    for side in range(2):
        groups = []
        for group in range(4):
            merged = jnp.zeros((8, 128), F32)
            for spot in range(4):
                moved = pack_in[4 * side + spot]
                shift = (32 * (spot - group)) % 128
                if shift:
                    moved = pltpu.roll(moved, shift, 1)
                merged = jnp.where(lane // 32 == spot, moved, merged)
            groups.append(merged)
        halves.append(jnp.concatenate(groups, axis=0))
    slab_high, slab_low = split(jnp.concatenate(halves, axis=1))
    factors = mm(slab_high, table[7]) + mm(slab_low, table[7])
    lanes = lax.broadcasted_iota(jnp.int32, (PAIR, HALF), 1)
    subs = lax.broadcasted_iota(jnp.int32, (PAIR, HALF), 0)

    def convolve(part):
        even = factors[PART * part : PART * part + PAIR]
        odd = factors[PART * part + PAIR : PART * (part + 1)]
        gain_cc = even[:, :HALF]
        gain_cs = jnp.where(lanes == 0, even[:, HALF:], gain_cc)
        gain_sc, gain_ss, edge = gain_cc, gain_cs, lanes == 0
        if part == 0:
            special = jnp.logical_and(subs == 0, chip == 0)
            gain_sc = jnp.where(special, odd[:, :HALF], gain_cc)
            gain_ss = jnp.where(special, jnp.where(lanes == 0, odd[:, HALF:], odd[:, :HALF]), gain_cs)
            edge = jnp.logical_or(special, lanes == 0)
        mixing = jnp.where(edge, 0.0, odd[:, HALF:])
        slab = rows_out[pl.ds(pl.multiple_of(HALF * part + PART * chip, PART), PART), :].astype(F32)
        for step in range(1, CHIPS):
            slab = slab + rows_in[part, step].astype(F32)
        spectrum = mm3(split(slab), (to_cols[0][...], to_cols[1][...]))
        part_cc, part_cs = spectrum[:PAIR, :HALF], spectrum[:PAIR, HALF:]
        part_sc, part_ss = spectrum[PAIR:, :HALF], spectrum[PAIR:, HALF:]
        spec_out[part, :PAIR, :HALF] = gain_cc * part_cc - mixing * part_ss
        spec_out[part, :PAIR, HALF:] = gain_cs * part_cs + mixing * part_sc
        spec_out[part, PAIR:, :HALF] = gain_sc * part_sc + mixing * part_cs
        spec_out[part, PAIR:, HALF:] = gain_ss * part_ss - mixing * part_cc

    spectra = [[] for _ in range(HALVES)]
    for part in range(HALVES):
        for copy in sums[part]:
            copy.wait_recv()
        convolve(part)
        if part == 0:

            @pl.when(jnp.logical_not(leads))
            def _():
                pl.semaphore_wait(met_in, 1)

        for step in (4, 3, 2, 1, 0):
            copy = pltpu.make_async_remote_copy(
                src_ref=spec_out.at[part],
                dst_ref=spec_in.at[part, step],
                send_sem=spec_send.at[part, step],
                recv_sem=spec_recv.at[part, step],
                device_id=meets(step),
                device_id_type=MESH,
            )
            copy.start()
            spectra[part].append(copy)

    gains = [stop[s] for s in range(STOPS)]
    weights = [stop[s] * para[s] for s in range(STOPS)]
    marks_up = [marks[2 * core, s].astype(F32) for s in range(STOPS)]
    marks_down = [marks[2 * core + 1, s].astype(F32) for s in range(STOPS)]
    column = lax.broadcasted_iota(jnp.int32, (PART, GRID), 1)

    def encounter(three):
        moved_up = jnp.where(column >= OFFSET_CELLS, pltpu.roll(three[PART : 2 * PART], OFFSET_CELLS, 1), 0.0)
        moved_down = jnp.where(
            column < GRID - OFFSET_CELLS, pltpu.roll(three[2 * PART :], GRID - OFFSET_CELLS, 1), 0.0
        )
        return three[:PART] + moved_up + moved_down

    def collect(part):
        direct = jnp.zeros((PART, GRID), F32)
        upward = jnp.zeros((PART, GRID), F32)
        downward = jnp.zeros((PART, GRID), F32)
        for step in range(STOPS + 1):
            partner = spec_in[part, step]
            if step < STOPS:
                direct = direct + gains[step] * partner
            if step >= 1:
                upward = upward + (weights[step - 1] * marks_up[step - 1]) * partner
            if step + 1 < STOPS:
                downward = downward + (weights[step + 1] * marks_down[step + 1]) * partner
        mixed = mm3(
            split(jnp.concatenate([direct, upward, downward], axis=0)),
            (from_cols[0][...], from_cols[1][...]),
        )
        smooth = encounter(mixed)
        sine = sines[pl.ds(pl.multiple_of(PAIR * (HALVES * chip + part), PAIR), PAIR), :]
        sine = jnp.concatenate([sine, sine], axis=1)
        along_x = jnp.concatenate([-sine * smooth[PAIR:], sine * smooth[:PAIR]], axis=0)
        along_y = encounter(-0.5 * (pltpu.roll(mixed, GRID - 1, 1) - pltpu.roll(mixed, 1, 1)))
        return jnp.concatenate([along_x, along_y], axis=1).astype(BF16)

    gathers = [[] for _ in range(HALVES)]
    for part in range(HALVES):
        for copy in spectra[part]:
            copy.wait_recv()
        mine = pl.ds(pl.multiple_of(HALF * part + PART * chip, PART), PART)
        total[mine, :] = collect(part)
        for step in RING_ORDER:
            there, device = ring(step)
            copy = pltpu.make_async_remote_copy(
                src_ref=total.at[mine],
                dst_ref=total.at[mine],
                send_sem=total_send.at[part, step],
                recv_sem=total_recv.at[part, step],
                device_id=device,
                device_id_type=MESH,
            )
            copy.start()
            gathers[part].append(copy)
    def kicks(part, half, turned, target):
        for first in range(0, parts, CHUNK):
            values = mm(turned, row_wave[part, :, pl.ds(half * parts + first, CHUNK)])
            hit = cell_iota == cells[half, 1:2, first : first + CHUNK]
            for axis in range(2):
                picked = jnp.where(hit, values[axis * GRID : (axis + 1) * GRID], 0.0)
                target(half, axis, first, jnp.sum(picked, axis=0, keepdims=True))

    def turn(part):
        for copy in gathers[part]:
            copy.wait_recv()
        rows = jnp.transpose(total[HALF * part : HALF * (part + 1), :].astype(F32)).astype(BF16)
        return jnp.concatenate([rows, rows], axis=1)

    def keep(half, axis, first, value):
        kick_first[half, axis : axis + 1, first : first + CHUNK] = value

    def to_sibling(half, axis, first, value):
        before = kick_first[half, axis : axis + 1, first : first + CHUNK]
        kick_out[axis : axis + 1, first : first + CHUNK] = before + value

    def to_output(half, axis, first, value):
        before = kick_first[half, axis : axis + 1, first : first + CHUNK]
        out_ref[core, 0, axis : axis + 1, first : first + CHUNK] = (
            momenta[core, 0, axis : axis + 1, first : first + CHUNK] + (before + value)
        )

    turned = turn(0)
    kicks(0, 1, turned, keep)
    kicks(0, 0, turned, keep)
    turned = turn(1)
    kicks(1, 1, turned, to_sibling)
    back = pltpu.make_async_remote_copy(
        src_ref=kick_out,
        dst_ref=kick_in,
        send_sem=kick_send,
        recv_sem=kick_recv,
        device_id=sibling,
        device_id_type=MESH,
    )
    back.start()
    kicks(1, 0, turned, to_output)
    back.wait_recv()
    out_ref[other, 0] = momenta[other, 0] + kick_in[...]
    for copy in [*swaps, *packs, *sums[0], *sums[1], *spectra[0], *spectra[1], *gathers[0], *gathers[1], back]:
        copy.wait_send()


def body(bunches, tables, *operands):
    cell_index, charges, momenta, fill_pattern, encounters, green_spectrum, stop_gain, parasitic_gain = operands
    parts = cell_index.shape[3]
    stacked, sines = tables
    charges = charges.reshape(2, parts)
    fill_pattern = fill_pattern.reshape(2)
    encounters = encounters.reshape(STOPS, 2, 2).transpose(1, 2, 0).reshape(4, STOPS)
    green_spectrum = green_spectrum.T
    operands = (cell_index, charges, momenta, fill_pattern, encounters, green_spectrum, stop_gain, parasitic_gain)
    any_spec = pl.BlockSpec(memory_space=pltpu.HBM)
    dma = pltpu.SemaphoreType.DMA
    return pl.pallas_call(
        functools.partial(kernel, bunches),
        out_shape=jax.ShapeDtypeStruct(momenta.shape, F32),
        in_specs=[any_spec] * 10,
        out_specs=pl.BlockSpec(memory_space=pltpu.VMEM),
        scratch_shapes=[
            pltpu.VMEM((2, 2, parts), jnp.int32),
            pltpu.VMEM((2, parts), BF16),
            pltpu.VMEM((2, parts), BF16),
            pltpu.VMEM((2, 1, 2, parts), F32),
            pltpu.SMEM(fill_pattern.shape, jnp.int32),
            pltpu.SMEM(encounters.shape, jnp.int32),
            pltpu.VMEM(green_spectrum.shape, F32),
            pltpu.SMEM(stop_gain.shape, F32),
            pltpu.SMEM(parasitic_gain.shape, F32),
            pltpu.VMEM(stacked.shape, BF16),
            pltpu.VMEM(sines.shape, F32),
            pltpu.VMEM((128, GRID), F32),
            pltpu.VMEM((CHIPS, 8, 128), F32),
            pltpu.VMEM((CHIPS, 8, 128), F32),
            pltpu.VMEM((CHIPS, 8, 128), F32),
            pltpu.VMEM((CHIPS, 8, 128), F32),
            pltpu.VMEM((GRID, 2 * parts), BF16),
            pltpu.VMEM((GRID, 2 * parts), BF16),
            pltpu.VMEM((HALVES, GRID, 2 * parts), BF16),
            pltpu.VMEM((2, 2, parts), F32),
            pltpu.VMEM((GRID, GRID), BF16),
            pltpu.VMEM((HALVES, CHIPS, PART, GRID), BF16),
            pltpu.VMEM((HALVES, PART, GRID), F32),
            pltpu.VMEM((HALVES, STOPS + 1, PART, GRID), F32),
            pltpu.VMEM((GRID, 2 * GRID), BF16),
            pltpu.VMEM((2, parts), F32),
            pltpu.VMEM((2, parts), F32),
            dma((10,)),
            dma((3,)),
            dma((3,)),
            dma((CHIPS,)),
            dma((CHIPS,)),
            dma((HALVES, CHIPS)),
            dma((HALVES, CHIPS)),
            dma((HALVES, STOPS + 1)),
            dma((HALVES, STOPS + 1)),
            dma((HALVES, CHIPS)),
            dma((HALVES, CHIPS)),
            dma(()),
            dma(()),
            pltpu.SemaphoreType.REGULAR,
            pltpu.SemaphoreType.REGULAR,
        ],
        compiler_params=pltpu.CompilerParams(
            collective_id=0, has_side_effects=True, vmem_limit_bytes=60 << 20
        ),
    )(*operands, stacked, sines)


def solution(mesh):
    in_specs = (
        P(None, "bunch", None, "tile"),
        P(None, "bunch", "tile"),
        P(None, "bunch", None, "tile"),
        P(None, "bunch"),
        P(None, None, None, "bunch"),
        P(None, "tile"),
        P(),
        P(),
    )
    out_specs = P(None, "bunch", None, "tile")
    tables = make_tables()
    return jax.shard_map(
        functools.partial(body, mesh.shape["bunch"], tables),
        mesh=mesh,
        in_specs=in_specs,
        out_specs=out_specs,
        check_vma=False,
    )
```

```python
import functools
import math

import jax
import jax.numpy as jnp
import ml_dtypes
import numpy as np
from jax import lax
from jax.experimental import pallas as pl
from jax.experimental.pallas import tpu as pltpu
from jax.sharding import PartitionSpec as P

GRID = 256
HALF = GRID // 2
STOPS = 4
OFFSET_CELLS = 32
CHIPS = 8
SLAB = GRID // CHIPS
HALVES = 2
PART = SLAB // HALVES
PAIR = PART // 2
CHUNK = 256
LEAD = 4
MESH = pl.DeviceIdType.MESH
F32 = jnp.float32
BF16 = jnp.bfloat16
RING_ORDER = (4, 3, 5, 2, 6, 1, 7)


def split_np(table):
    high = table.astype(ml_dtypes.bfloat16)
    low = (table - high.astype(np.float64)).astype(ml_dtypes.bfloat16)
    return high, low


def basis_rows(wave, is_sine):
    positions = np.arange(GRID)
    if is_sine and wave == 0:
        return np.cos(math.pi * positions) / 16.0
    if wave == 0:
        return np.full(GRID, 1.0 / 16.0)
    angle = 2.0 * math.pi / GRID * ((wave * positions) % GRID)
    return (np.sin(angle) if is_sine else np.cos(angle)) * math.sqrt(2.0) / 16.0


def fold_row(wave, is_sine):
    row = np.zeros(GRID)
    if wave == 0:
        row[HALF if is_sine else 0] = 1.0
    else:
        row[wave] = 0.5
        row[GRID - wave] = -0.5 if is_sine else 0.5
    return row


def make_tables():
    slab_order = [
        (PAIR * part + r % PAIR, r >= PAIR) for part in range(CHIPS * HALVES) for r in range(PART)
    ]
    half_order = [
        slab_order[SLAB * chip + PART * part + r]
        for part in range(HALVES)
        for chip in range(CHIPS)
        for r in range(PART)
    ]
    plain_order = [(q % HALF, q >= HALF) for q in range(GRID)]
    row_basis = np.stack([basis_rows(*entry) for entry in half_order])
    col_basis = np.stack([basis_rows(*entry) for entry in plain_order])
    row_fold = np.stack([fold_row(*entry) for entry in slab_order])
    col_fold = np.stack([fold_row(*entry) for entry in plain_order]).T
    stacked = np.stack(
        [
            *split_np(row_basis),
            *split_np(col_basis.T),
            *split_np(col_basis),
            row_fold.astype(ml_dtypes.bfloat16),
            col_fold.astype(ml_dtypes.bfloat16),
        ]
    )
    sines = np.sin(2.0 * math.pi / GRID * np.arange(HALF))
    return stacked, np.repeat(sines[:, None], 128, axis=1).astype(np.float32)


def split(value):
    high = value.astype(BF16)
    return high, (value - high.astype(F32)).astype(BF16)


def mm(a, b):
    return jnp.dot(a, b, preferred_element_type=F32)


def mm_nt(a, b):
    return lax.dot_general(a, b, (((1,), (1,)), ((), ())), preferred_element_type=F32)


def mm3(a, b):
    return mm(a[0], b[0]) + (mm(a[0], b[1]) + mm(a[1], b[0]))


def kernel(
    bunches,
    cell_ref,
    charge_ref,
    fill_ref,
    mark_ref,
    green_ref,
    stop_ref,
    para_ref,
    table_ref,
    sine_ref,
    out_ref,
    cells,
    charge,
    charge_other,
    fill,
    marks,
    green,
    stop,
    para,
    table,
    sines,
    wide,
    pack_mine,
    pack_other,
    pack_out,
    pack_in,
    row_hot,
    col_hot,
    col_plain,
    row_wave,
    kick_first,
    rows_out,
    rows_in,
    spec_out,
    spec_in,
    total,
    kick_out,
    kick_own,
    load_sem,
    swap_send,
    swap_recv,
    pack_send,
    pack_recv,
    rows_send,
    rows_recv,
    spec_send,
    spec_recv,
    total_send,
    total_recv,
    kick_send,
    kick_recv,
    own_sem,
    ring_in,
    met_in,
):
    parts = cells.shape[2]
    bunch = lax.axis_index("bunch")
    tile = lax.axis_index("tile")
    chip = lax.div(tile, 2)
    core = lax.rem(tile, 2)
    other = 1 - core
    sibling = (bunch, 2 * chip + other)

    def ring(step):
        there = lax.rem(chip + step, CHIPS)
        return there, (bunch, 2 * there + core)

    def meets(step):
        return (lax.rem(bunch + (1 - 2 * core) * step + 4 * bunches, bunches), 2 * chip + other)

    barrier = pltpu.get_barrier_semaphore()
    leads = lax.rem(chip, LEAD) == 0
    near = [sibling] + [ring(step)[1] for step in range(1, CHIPS)]
    for partner in near:
        pl.semaphore_signal(barrier, inc=1, device_id=partner, device_id_type=MESH)

    @pl.when(leads)
    def _():
        for step in range(1, STOPS + 1):
            pl.semaphore_signal(barrier, inc=1, device_id=meets(step), device_id_type=MESH)

    loads = [
        pltpu.make_async_copy(source, target, load_sem.at[index])
        for index, (source, target) in enumerate(
            [
                (green_ref, green),
                (table_ref, table),
                (cell_ref.at[core, 0], cells.at[0]),
                (charge_ref, charge),
                (fill_ref, fill),
                (mark_ref, marks),
                (stop_ref, stop),
                (para_ref, para),
                (sine_ref, sines),
            ]
        )
    ]
    for load in loads:
        load.start()

    row_basis = (table.at[0], table.at[1])
    to_cols = (table.at[2], table.at[3])
    from_cols = (table.at[4], table.at[5])

    loads[0].wait()
    loads[1].wait()
    wide[...] = jnp.zeros(wide.shape, F32)
    wide[0 : green.shape[0]] = green[...]
    green_high, green_low = split(wide[...])
    folded = mm_nt(table[6], green_high) + mm_nt(table[6], green_low)
    folded = folded.reshape(CHIPS, 4, 8, 128)
    packed = folded[:, 0].reshape(CHIPS * 8, 128)
    for group in range(1, 4):
        packed = packed + pltpu.roll(folded[:, group].reshape(CHIPS * 8, 128), 32 * group, 1)
    packed = pltpu.roll(packed, 16 * core, 1)
    pack_mine[...] = packed.reshape(CHIPS, 8, 128)

    pl.semaphore_wait(barrier, jnp.where(leads, len(near) + STOPS, len(near)))

    @pl.when(leads)
    def _():
        for step in range(1, STOPS + 1):
            pl.semaphore_signal(ring_in, inc=1, device_id=meets(step), device_id_type=MESH)

    swaps = [
        pltpu.make_async_remote_copy(
            src_ref=source,
            dst_ref=target,
            send_sem=swap_send.at[index],
            recv_sem=swap_recv.at[index],
            device_id=sibling,
            device_id_type=MESH,
        )
        for index, (source, target) in enumerate(
            [
                (cell_ref.at[other, 0], cells.at[1]),
                (charge_ref, charge_other),
                (pack_mine, pack_other),
            ]
        )
    ]
    for swap in swaps:
        swap.start()

    cell_iota = lax.broadcasted_iota(jnp.int32, (GRID, CHUNK), 0)

    def deposit(half):
        filled = fill[core].astype(F32)
        for first in range(0, parts, CHUNK):
            here = pl.ds(half * parts + first, CHUNK)
            rows = cells[half, 0:1, first : first + CHUNK]
            cols = cells[half, 1:2, first : first + CHUNK]
            both = (charge, charge_other)[half][:, first : first + CHUNK].astype(F32)
            weight = jnp.where(core == 0, both[0:1], both[1:2]) * filled
            row_hot[:, here] = jnp.where(cell_iota == rows, 1.0, 0.0).astype(BF16)
            col_hot[:, here] = jnp.where(cell_iota == cols, weight, 0.0).astype(BF16)
        span = pl.ds(half * parts, parts)
        return mm_nt(row_hot[:, span], col_hot[:, span])

    for load in loads[2:]:
        load.wait()
    density = deposit(0)
    for swap in swaps:
        swap.wait_recv()

    pack_out[...] = pack_mine[...] + pack_other[...]
    pack_in[chip] = pack_out[chip]
    packs = []
    for step in RING_ORDER:
        there, device = ring(step)
        copy = pltpu.make_async_remote_copy(
            src_ref=pack_out.at[there],
            dst_ref=pack_in.at[chip],
            send_sem=pack_send.at[step],
            recv_sem=pack_recv.at[step],
            device_id=device,
            device_id_type=MESH,
        )
        copy.start()
        packs.append(copy)

    density = density + deposit(1)
    basis_high, basis_low = row_basis[0][...], row_basis[1][...]
    pieces = split(density)
    partial = mm3((basis_high[:HALF], basis_low[:HALF]), pieces)
    rows_out[:HALF, :] = partial.astype(BF16)
    top = partial[0:16]
    first_row = lax.broadcasted_iota(jnp.int32, top.shape, 0) == 0
    rows_out[0:16, :] = jnp.where(first_row, top - jnp.mean(top, axis=1, keepdims=True), top).astype(BF16)
    sums = [[] for _ in range(HALVES)]
    for part in range(HALVES):
        if part == 1:
            rows_out[HALF:, :] = mm3((basis_high[HALF:], basis_low[HALF:]), pieces).astype(BF16)
        for step in RING_ORDER:
            there, device = ring(step)
            first = pl.multiple_of(HALF * part + PART * there, PART)
            copy = pltpu.make_async_remote_copy(
                src_ref=rows_out.at[pl.ds(first, PART)],
                dst_ref=rows_in.at[part, step],
                send_sem=rows_send.at[part, step],
                recv_sem=rows_recv.at[part, step],
                device_id=device,
                device_id_type=MESH,
            )
            copy.start()
            sums[part].append(copy)

    for first in range(0, 2 * parts, CHUNK):
        here = pl.ds(first, CHUNK)
        row_wave[:, here] = mm(basis_high, row_hot[:, here]) + mm(basis_low, row_hot[:, here])
        cols = cells[first // parts, 1:2, first % parts : first % parts + CHUNK]
        col_plain[:, here] = jnp.where(cell_iota == cols, 1.0, 0.0).astype(BF16)

    @pl.when(leads)
    def _():
        pl.semaphore_wait(ring_in, STOPS)
        for ahead in range(1, LEAD):
            follower = (bunch, 2 * (chip + ahead) + core)
            pl.semaphore_signal(met_in, inc=1, device_id=follower, device_id_type=MESH)

    for copy in packs:
        copy.wait_recv()
    lane = lax.broadcasted_iota(jnp.int32, (8, 128), 1)
    halves = []
    for side in range(2):
        groups = []
        for group in range(4):
            merged = jnp.zeros((8, 128), F32)
            for spot in range(4):
                moved = pack_in[4 * side + spot]
                shift = (32 * (spot - group)) % 128
                if shift:
                    moved = pltpu.roll(moved, shift, 1)
                merged = jnp.where(lane // 32 == spot, moved, merged)
            groups.append(merged)
        halves.append(jnp.concatenate(groups, axis=0))
    slab_high, slab_low = split(jnp.concatenate(halves, axis=1))
    factors = mm(slab_high, table[7]) + mm(slab_low, table[7])
    lanes = lax.broadcasted_iota(jnp.int32, (PAIR, HALF), 1)
    subs = lax.broadcasted_iota(jnp.int32, (PAIR, HALF), 0)

    def convolve(part):
        even = factors[PART * part : PART * part + PAIR]
        odd = factors[PART * part + PAIR : PART * (part + 1)]
        gain_cc = even[:, :HALF]
        gain_cs = jnp.where(lanes == 0, even[:, HALF:], gain_cc)
        gain_sc, gain_ss, edge = gain_cc, gain_cs, lanes == 0
        if part == 0:
            special = jnp.logical_and(subs == 0, chip == 0)
            gain_sc = jnp.where(special, odd[:, :HALF], gain_cc)
            gain_ss = jnp.where(special, jnp.where(lanes == 0, odd[:, HALF:], odd[:, :HALF]), gain_cs)
            edge = jnp.logical_or(special, lanes == 0)
        mixing = jnp.where(edge, 0.0, odd[:, HALF:])
        slab = rows_out[pl.ds(pl.multiple_of(HALF * part + PART * chip, PART), PART), :].astype(F32)
        for step in range(1, CHIPS):
            slab = slab + rows_in[part, step].astype(F32)
        spectrum = mm3(split(slab), (to_cols[0][...], to_cols[1][...]))
        part_cc, part_cs = spectrum[:PAIR, :HALF], spectrum[:PAIR, HALF:]
        part_sc, part_ss = spectrum[PAIR:, :HALF], spectrum[PAIR:, HALF:]
        spec_out[part, :PAIR, :HALF] = gain_cc * part_cc - mixing * part_ss
        spec_out[part, :PAIR, HALF:] = gain_cs * part_cs + mixing * part_sc
        spec_out[part, PAIR:, :HALF] = gain_sc * part_sc + mixing * part_cs
        spec_out[part, PAIR:, HALF:] = gain_ss * part_ss - mixing * part_cc

    spectra = [[] for _ in range(HALVES)]
    for part in range(HALVES):
        for copy in sums[part]:
            copy.wait_recv()
        convolve(part)
        if part == 0:

            @pl.when(jnp.logical_not(leads))
            def _():
                pl.semaphore_wait(met_in, 1)

        for step in (4, 3, 2, 1, 0):
            copy = pltpu.make_async_remote_copy(
                src_ref=spec_out.at[part],
                dst_ref=spec_in.at[part, step],
                send_sem=spec_send.at[part, step],
                recv_sem=spec_recv.at[part, step],
                device_id=meets(step),
                device_id_type=MESH,
            )
            copy.start()
            spectra[part].append(copy)

    gains = [stop[s] for s in range(STOPS)]
    weights = [stop[s] * para[s] for s in range(STOPS)]
    marks_up = [marks[2 * core, s].astype(F32) for s in range(STOPS)]
    marks_down = [marks[2 * core + 1, s].astype(F32) for s in range(STOPS)]
    column = lax.broadcasted_iota(jnp.int32, (PART, GRID), 1)

    def encounter(three):
        moved_up = jnp.where(column >= OFFSET_CELLS, pltpu.roll(three[PART : 2 * PART], OFFSET_CELLS, 1), 0.0)
        moved_down = jnp.where(
            column < GRID - OFFSET_CELLS, pltpu.roll(three[2 * PART :], GRID - OFFSET_CELLS, 1), 0.0
        )
        return three[:PART] + moved_up + moved_down

    def collect(part):
        direct = jnp.zeros((PART, GRID), F32)
        upward = jnp.zeros((PART, GRID), F32)
        downward = jnp.zeros((PART, GRID), F32)
        for step in range(STOPS + 1):
            partner = spec_in[part, step]
            if step < STOPS:
                direct = direct + gains[step] * partner
            if step >= 1:
                upward = upward + (weights[step - 1] * marks_up[step - 1]) * partner
            if step + 1 < STOPS:
                downward = downward + (weights[step + 1] * marks_down[step + 1]) * partner
        mixed = mm3(
            split(jnp.concatenate([direct, upward, downward], axis=0)),
            (from_cols[0][...], from_cols[1][...]),
        )
        smooth = encounter(mixed)
        sine = sines[pl.ds(pl.multiple_of(PAIR * (HALVES * chip + part), PAIR), PAIR), :]
        sine = jnp.concatenate([sine, sine], axis=1)
        along_x = jnp.concatenate([-sine * smooth[PAIR:], sine * smooth[:PAIR]], axis=0)
        along_y = encounter(-0.5 * (pltpu.roll(mixed, GRID - 1, 1) - pltpu.roll(mixed, 1, 1)))
        return jnp.concatenate([along_x, along_y], axis=1).astype(BF16)

    gathers = [[] for _ in range(HALVES)]
    for part in range(HALVES):
        for copy in spectra[part]:
            copy.wait_recv()
        mine = pl.ds(pl.multiple_of(HALF * part + PART * chip, PART), PART)
        total[mine, :] = collect(part)
        for place in range(CHIPS - 1):
            there = place + jnp.where(place >= chip, 1, 0)
            step = lax.rem(there - chip + CHIPS, CHIPS)
            copy = pltpu.make_async_remote_copy(
                src_ref=total.at[mine],
                dst_ref=total.at[mine],
                send_sem=total_send.at[part, place],
                recv_sem=total_recv.at[part, step],
                device_id=(bunch, 2 * there + core),
                device_id_type=MESH,
            )
            copy.start()
            gathers[part].append(copy)
    def kicks(part, half, target):
        span = slice(HALF * part, HALF * (part + 1))
        stacked = jnp.concatenate([total[span, :GRID], total[span, GRID:]], axis=0)
        for first in range(0, parts, CHUNK):
            here = pl.ds(half * parts + first, CHUNK)
            values = mm(stacked, col_plain[:, here])
            wave = row_wave[span, here]
            for axis in range(2):
                picked = values[axis * HALF : (axis + 1) * HALF] * wave
                target(half, axis, first, jnp.sum(picked, axis=0, keepdims=True))

    def arrive(part):
        mine = pl.ds(pl.multiple_of(HALF * part + PART * chip, PART), PART)
        for step in range(1, CHIPS):
            pltpu.make_async_remote_copy(
                src_ref=total.at[mine],
                dst_ref=total.at[mine],
                send_sem=total_send.at[part, 0],
                recv_sem=total_recv.at[part, step],
                device_id=ring(step)[1],
                device_id_type=MESH,
            ).wait_recv()

    def keep(half, axis, first, value):
        kick_first[half, axis : axis + 1, first : first + CHUNK] = value

    def to_sibling(half, axis, first, value):
        before = kick_first[half, axis : axis + 1, first : first + CHUNK]
        kick_out[axis : axis + 1, first : first + CHUNK] = before + value

    def to_output(half, axis, first, value):
        before = kick_first[half, axis : axis + 1, first : first + CHUNK]
        kick_own[axis : axis + 1, first : first + CHUNK] = before + value

    arrive(0)
    kicks(0, 1, keep)
    kicks(0, 0, keep)
    arrive(1)
    kicks(1, 1, to_sibling)
    back = pltpu.make_async_remote_copy(
        src_ref=kick_out,
        dst_ref=out_ref.at[core, 0],
        send_sem=kick_send,
        recv_sem=kick_recv,
        device_id=sibling,
        device_id_type=MESH,
    )
    back.start()
    kicks(1, 0, to_output)
    here = pltpu.make_async_copy(kick_own, out_ref.at[core, 0], own_sem)
    here.start()
    here.wait()
    back.wait_recv()
    for copy in [*swaps, *packs, *sums[0], *sums[1], *spectra[0], *spectra[1], *gathers[0], *gathers[1], back]:
        copy.wait_send()


def body(bunches, tables, *operands):
    cell_index, charges, momenta, fill_pattern, encounters, green_spectrum, stop_gain, parasitic_gain = operands
    parts = cell_index.shape[3]
    stacked, sines = tables
    charges = charges.reshape(2, parts)
    fill_pattern = fill_pattern.reshape(2)
    encounters = encounters.reshape(STOPS, 2, 2).transpose(1, 2, 0).reshape(4, STOPS)
    green_spectrum = green_spectrum.T
    operands = (cell_index, charges, fill_pattern, encounters, green_spectrum, stop_gain, parasitic_gain)
    any_spec = pl.BlockSpec(memory_space=pltpu.HBM)
    dma = pltpu.SemaphoreType.DMA
    kicks = pl.pallas_call(
        functools.partial(kernel, bunches),
        out_shape=jax.ShapeDtypeStruct(momenta.shape, F32),
        in_specs=[any_spec] * 9,
        out_specs=any_spec,
        scratch_shapes=[
            pltpu.VMEM((2, 2, parts), jnp.int32),
            pltpu.VMEM((2, parts), BF16),
            pltpu.VMEM((2, parts), BF16),
            pltpu.SMEM(fill_pattern.shape, jnp.int32),
            pltpu.SMEM(encounters.shape, jnp.int32),
            pltpu.VMEM(green_spectrum.shape, F32),
            pltpu.SMEM(stop_gain.shape, F32),
            pltpu.SMEM(parasitic_gain.shape, F32),
            pltpu.VMEM(stacked.shape, BF16),
            pltpu.VMEM(sines.shape, F32),
            pltpu.VMEM((128, GRID), F32),
            pltpu.VMEM((CHIPS, 8, 128), F32),
            pltpu.VMEM((CHIPS, 8, 128), F32),
            pltpu.VMEM((CHIPS, 8, 128), F32),
            pltpu.VMEM((CHIPS, 8, 128), F32),
            pltpu.VMEM((GRID, 2 * parts), BF16),
            pltpu.VMEM((GRID, 2 * parts), BF16),
            pltpu.VMEM((GRID, 2 * parts), BF16),
            pltpu.VMEM((GRID, 2 * parts), F32),
            pltpu.VMEM((2, 2, parts), F32),
            pltpu.VMEM((GRID, GRID), BF16),
            pltpu.VMEM((HALVES, CHIPS, PART, GRID), BF16),
            pltpu.VMEM((HALVES, PART, GRID), F32),
            pltpu.VMEM((HALVES, STOPS + 1, PART, GRID), F32),
            pltpu.VMEM((GRID, 2 * GRID), BF16),
            pltpu.VMEM((2, parts), F32),
            pltpu.VMEM((2, parts), F32),
            dma((9,)),
            dma((3,)),
            dma((3,)),
            dma((CHIPS,)),
            dma((CHIPS,)),
            dma((HALVES, CHIPS)),
            dma((HALVES, CHIPS)),
            dma((HALVES, STOPS + 1)),
            dma((HALVES, STOPS + 1)),
            dma((HALVES, CHIPS)),
            dma((HALVES, CHIPS)),
            dma(()),
            dma(()),
            dma(()),
            pltpu.SemaphoreType.REGULAR,
            pltpu.SemaphoreType.REGULAR,
        ],
        compiler_params=pltpu.CompilerParams(
            collective_id=0, has_side_effects=True, vmem_limit_bytes=60 << 20
        ),
    )(*operands, stacked, sines)
    return momenta + kicks


def solution(mesh):
    in_specs = (
        P(None, "bunch", None, "tile"),
        P(None, "bunch", "tile"),
        P(None, "bunch", None, "tile"),
        P(None, "bunch"),
        P(None, None, None, "bunch"),
        P(None, "tile"),
        P(),
        P(),
    )
    out_specs = P(None, "bunch", None, "tile")
    tables = make_tables()
    return jax.shard_map(
        functools.partial(body, mesh.shape["bunch"], tables),
        mesh=mesh,
        in_specs=in_specs,
        out_specs=out_specs,
        check_vma=False,
    )
```

```python
import functools
import math

import jax
import jax.numpy as jnp
import ml_dtypes
import numpy as np
from jax import lax
from jax.experimental import pallas as pl
from jax.experimental.pallas import tpu as pltpu
from jax.sharding import PartitionSpec as P

GRID = 256
HALF = GRID // 2
STOPS = 4
OFFSET_CELLS = 32
CHIPS = 8
SLAB = GRID // CHIPS
HALVES = 2
PART = SLAB // HALVES
PAIR = PART // 2
CHUNK = 256
LEAD = 4
MESH = pl.DeviceIdType.MESH
F32 = jnp.float32
BF16 = jnp.bfloat16
RING_ORDER = (4, 3, 5, 2, 6, 1, 7)


def split_np(table):
    high = table.astype(ml_dtypes.bfloat16)
    low = (table - high.astype(np.float64)).astype(ml_dtypes.bfloat16)
    return high, low


def basis_rows(wave, is_sine):
    positions = np.arange(GRID)
    if is_sine and wave == 0:
        return np.cos(math.pi * positions) / 16.0
    if wave == 0:
        return np.full(GRID, 1.0 / 16.0)
    angle = 2.0 * math.pi / GRID * ((wave * positions) % GRID)
    return (np.sin(angle) if is_sine else np.cos(angle)) * math.sqrt(2.0) / 16.0


def fold_row(wave, is_sine):
    row = np.zeros(GRID)
    if wave == 0:
        row[HALF if is_sine else 0] = 1.0
    else:
        row[wave] = 0.5
        row[GRID - wave] = -0.5 if is_sine else 0.5
    return row


def make_tables():
    slab_order = [
        (PAIR * part + r % PAIR, r >= PAIR) for part in range(CHIPS * HALVES) for r in range(PART)
    ]
    half_order = [
        slab_order[SLAB * chip + PART * part + r]
        for part in range(HALVES)
        for chip in range(CHIPS)
        for r in range(PART)
    ]
    plain_order = [(q % HALF, q >= HALF) for q in range(GRID)]
    row_basis = np.stack([basis_rows(*entry) for entry in half_order])
    col_basis = np.stack([basis_rows(*entry) for entry in plain_order])
    row_fold = np.stack([fold_row(*entry) for entry in slab_order])
    col_fold = np.stack([fold_row(*entry) for entry in plain_order]).T
    stacked = np.stack(
        [
            *split_np(row_basis),
            *split_np(col_basis.T),
            *split_np(col_basis),
            row_fold.astype(ml_dtypes.bfloat16),
            col_fold.astype(ml_dtypes.bfloat16),
        ]
    )
    sines = np.sin(2.0 * math.pi / GRID * np.arange(HALF))
    return stacked, np.repeat(sines[:, None], 128, axis=1).astype(np.float32)


def split(value):
    high = value.astype(BF16)
    return high, (value - high.astype(F32)).astype(BF16)


def mm(a, b):
    return jnp.dot(a, b, preferred_element_type=F32)


def mm_nt(a, b):
    return lax.dot_general(a, b, (((1,), (1,)), ((), ())), preferred_element_type=F32)


def mm3(a, b):
    return mm(a[0], b[0]) + (mm(a[0], b[1]) + mm(a[1], b[0]))


def kernel(
    bunches,
    cell_ref,
    charge_ref,
    fill_ref,
    mark_ref,
    green_ref,
    stop_ref,
    para_ref,
    table_ref,
    sine_ref,
    out_ref,
    cells,
    charge,
    charge_other,
    fill,
    marks,
    green,
    stop,
    para,
    table,
    sines,
    wide,
    pack_mine,
    pack_other,
    pack_out,
    pack_in,
    row_hot,
    col_hot,
    col_plain,
    row_wave,
    kick_first,
    rows_out,
    rows_in,
    spec_out,
    spec_in,
    total,
    kick_out,
    kick_own,
    load_sem,
    swap_send,
    swap_recv,
    pack_send,
    pack_recv,
    rows_send,
    rows_recv,
    spec_send,
    spec_recv,
    total_send,
    total_recv,
    kick_send,
    kick_recv,
    own_sem,
    ring_in,
    met_in,
):
    parts = cells.shape[2]
    bunch = lax.axis_index("bunch")
    tile = lax.axis_index("tile")
    chip = lax.div(tile, 2)
    core = lax.rem(tile, 2)
    other = 1 - core
    sibling = (bunch, 2 * chip + other)

    def ring(step):
        there = lax.rem(chip + step, CHIPS)
        return there, (bunch, 2 * there + core)

    def meets(step):
        return (lax.rem(bunch + (1 - 2 * core) * step + 4 * bunches, bunches), 2 * chip + other)

    barrier = pltpu.get_barrier_semaphore()
    leads = lax.rem(chip, LEAD) == 0
    near = [sibling] + [ring(step)[1] for step in range(1, CHIPS)]
    for partner in near:
        pl.semaphore_signal(barrier, inc=1, device_id=partner, device_id_type=MESH)

    @pl.when(leads)
    def _():
        for step in range(1, STOPS + 1):
            pl.semaphore_signal(barrier, inc=1, device_id=meets(step), device_id_type=MESH)

    loads = [
        pltpu.make_async_copy(source, target, load_sem.at[index])
        for index, (source, target) in enumerate(
            [
                (green_ref, green),
                (table_ref, table),
                (cell_ref.at[core, 0], cells.at[0]),
                (charge_ref, charge),
                (fill_ref, fill),
                (mark_ref, marks),
                (stop_ref, stop),
                (para_ref, para),
                (sine_ref, sines),
            ]
        )
    ]
    for load in loads:
        load.start()

    row_basis = (table.at[0], table.at[1])
    to_cols = (table.at[2], table.at[3])
    from_cols = (table.at[4], table.at[5])

    loads[0].wait()
    loads[1].wait()
    wide[...] = jnp.zeros(wide.shape, F32)
    wide[0 : green.shape[0]] = green[...]
    green_high, green_low = split(wide[...])
    folded = mm_nt(table[6], green_high) + mm_nt(table[6], green_low)
    folded = folded.reshape(CHIPS, 4, 8, 128)
    packed = folded[:, 0].reshape(CHIPS * 8, 128)
    for group in range(1, 4):
        packed = packed + pltpu.roll(folded[:, group].reshape(CHIPS * 8, 128), 32 * group, 1)
    packed = pltpu.roll(packed, 16 * core, 1)
    pack_mine[...] = packed.reshape(CHIPS, 8, 128)

    pl.semaphore_wait(barrier, jnp.where(leads, len(near) + STOPS, len(near)))

    @pl.when(leads)
    def _():
        for step in range(1, STOPS + 1):
            pl.semaphore_signal(ring_in, inc=1, device_id=meets(step), device_id_type=MESH)

    swaps = [
        pltpu.make_async_remote_copy(
            src_ref=source,
            dst_ref=target,
            send_sem=swap_send.at[index],
            recv_sem=swap_recv.at[index],
            device_id=sibling,
            device_id_type=MESH,
        )
        for index, (source, target) in enumerate(
            [
                (cell_ref.at[other, 0], cells.at[1]),
                (charge_ref, charge_other),
                (pack_mine, pack_other),
            ]
        )
    ]
    for swap in swaps:
        swap.start()

    cell_iota = lax.broadcasted_iota(jnp.int32, (GRID, CHUNK), 0)

    def deposit(half):
        filled = fill[core].astype(F32)
        for first in range(0, parts, CHUNK):
            here = pl.ds(half * parts + first, CHUNK)
            rows = cells[half, 0:1, first : first + CHUNK]
            cols = cells[half, 1:2, first : first + CHUNK]
            both = (charge, charge_other)[half][:, first : first + CHUNK].astype(F32)
            weight = jnp.where(core == 0, both[0:1], both[1:2]) * filled
            row_hot[:, here] = jnp.where(cell_iota == rows, 1.0, 0.0).astype(BF16)
            col_hot[:, here] = jnp.where(cell_iota == cols, weight, 0.0).astype(BF16)
        span = pl.ds(half * parts, parts)
        return mm_nt(row_hot[:, span], col_hot[:, span])

    for load in loads[2:]:
        load.wait()
    density = deposit(0)
    for swap in swaps:
        swap.wait_recv()

    pack_out[...] = pack_mine[...] + pack_other[...]
    pack_in[chip] = pack_out[chip]
    packs = []
    for step in RING_ORDER:
        there, device = ring(step)
        copy = pltpu.make_async_remote_copy(
            src_ref=pack_out.at[there],
            dst_ref=pack_in.at[chip],
            send_sem=pack_send.at[step],
            recv_sem=pack_recv.at[step],
            device_id=device,
            device_id_type=MESH,
        )
        copy.start()
        packs.append(copy)

    density = density + deposit(1)
    basis_high, basis_low = row_basis[0][...], row_basis[1][...]
    pieces = split(density)
    partial = mm3((basis_high[:HALF], basis_low[:HALF]), pieces)
    rows_out[:HALF, :] = partial.astype(BF16)
    top = partial[0:16]
    first_row = lax.broadcasted_iota(jnp.int32, top.shape, 0) == 0
    rows_out[0:16, :] = jnp.where(first_row, top - jnp.mean(top, axis=1, keepdims=True), top).astype(BF16)
    sums = [[] for _ in range(HALVES)]
    for part in range(HALVES):
        if part == 1:
            rows_out[HALF:, :] = mm3((basis_high[HALF:], basis_low[HALF:]), pieces).astype(BF16)
        for step in RING_ORDER:
            there, device = ring(step)
            first = pl.multiple_of(HALF * part + PART * there, PART)
            copy = pltpu.make_async_remote_copy(
                src_ref=rows_out.at[pl.ds(first, PART)],
                dst_ref=rows_in.at[part, step],
                send_sem=rows_send.at[part, step],
                recv_sem=rows_recv.at[part, step],
                device_id=device,
                device_id_type=MESH,
            )
            copy.start()
            sums[part].append(copy)

    for first in range(0, 2 * parts, CHUNK):
        here = pl.ds(first, CHUNK)
        row_wave[:, here] = mm(basis_high, row_hot[:, here]) + mm(basis_low, row_hot[:, here])
        cols = cells[first // parts, 1:2, first % parts : first % parts + CHUNK]
        col_plain[:, here] = jnp.where(cell_iota == cols, 1.0, 0.0).astype(BF16)

    @pl.when(leads)
    def _():
        pl.semaphore_wait(ring_in, STOPS)
        for ahead in range(1, LEAD):
            follower = (bunch, 2 * (chip + ahead) + core)
            pl.semaphore_signal(met_in, inc=1, device_id=follower, device_id_type=MESH)

    for copy in packs:
        copy.wait_recv()
    lane = lax.broadcasted_iota(jnp.int32, (8, 128), 1)
    halves = []
    for side in range(2):
        groups = []
        for group in range(4):
            merged = jnp.zeros((8, 128), F32)
            for spot in range(4):
                moved = pack_in[4 * side + spot]
                shift = (32 * (spot - group)) % 128
                if shift:
                    moved = pltpu.roll(moved, shift, 1)
                merged = jnp.where(lane // 32 == spot, moved, merged)
            groups.append(merged)
        halves.append(jnp.concatenate(groups, axis=0))
    slab_high, slab_low = split(jnp.concatenate(halves, axis=1))
    factors = mm(slab_high, table[7]) + mm(slab_low, table[7])
    lanes = lax.broadcasted_iota(jnp.int32, (PAIR, HALF), 1)
    subs = lax.broadcasted_iota(jnp.int32, (PAIR, HALF), 0)

    def convolve(part):
        even = factors[PART * part : PART * part + PAIR]
        odd = factors[PART * part + PAIR : PART * (part + 1)]
        gain_cc = even[:, :HALF]
        gain_cs = jnp.where(lanes == 0, even[:, HALF:], gain_cc)
        gain_sc, gain_ss, edge = gain_cc, gain_cs, lanes == 0
        if part == 0:
            special = jnp.logical_and(subs == 0, chip == 0)
            gain_sc = jnp.where(special, odd[:, :HALF], gain_cc)
            gain_ss = jnp.where(special, jnp.where(lanes == 0, odd[:, HALF:], odd[:, :HALF]), gain_cs)
            edge = jnp.logical_or(special, lanes == 0)
        mixing = jnp.where(edge, 0.0, odd[:, HALF:])
        slab = rows_out[pl.ds(pl.multiple_of(HALF * part + PART * chip, PART), PART), :].astype(F32)
        for step in range(1, CHIPS):
            slab = slab + rows_in[part, step].astype(F32)
        spectrum = mm3(split(slab), (to_cols[0][...], to_cols[1][...]))
        part_cc, part_cs = spectrum[:PAIR, :HALF], spectrum[:PAIR, HALF:]
        part_sc, part_ss = spectrum[PAIR:, :HALF], spectrum[PAIR:, HALF:]
        spec_out[part, :PAIR, :HALF] = gain_cc * part_cc - mixing * part_ss
        spec_out[part, :PAIR, HALF:] = gain_cs * part_cs + mixing * part_sc
        spec_out[part, PAIR:, :HALF] = gain_sc * part_sc + mixing * part_cs
        spec_out[part, PAIR:, HALF:] = gain_ss * part_ss - mixing * part_cc

    spectra = [[] for _ in range(HALVES)]
    for part in range(HALVES):
        for copy in sums[part]:
            copy.wait_recv()
        convolve(part)
        if part == 0:

            @pl.when(jnp.logical_not(leads))
            def _():
                pl.semaphore_wait(met_in, 1)

        for step in (4, 3, 2, 1, 0):
            copy = pltpu.make_async_remote_copy(
                src_ref=spec_out.at[part],
                dst_ref=spec_in.at[part, step],
                send_sem=spec_send.at[part, step],
                recv_sem=spec_recv.at[part, step],
                device_id=meets(step),
                device_id_type=MESH,
            )
            copy.start()
            spectra[part].append(copy)

    gains = [stop[s] for s in range(STOPS)]
    weights = [stop[s] * para[s] for s in range(STOPS)]
    marks_up = [marks[2 * core, s].astype(F32) for s in range(STOPS)]
    marks_down = [marks[2 * core + 1, s].astype(F32) for s in range(STOPS)]
    column = lax.broadcasted_iota(jnp.int32, (PART, GRID), 1)

    def encounter(three):
        moved_up = jnp.where(column >= OFFSET_CELLS, pltpu.roll(three[PART : 2 * PART], OFFSET_CELLS, 1), 0.0)
        moved_down = jnp.where(
            column < GRID - OFFSET_CELLS, pltpu.roll(three[2 * PART :], GRID - OFFSET_CELLS, 1), 0.0
        )
        return three[:PART] + moved_up + moved_down

    def collect(part):
        direct = jnp.zeros((PART, GRID), F32)
        upward = jnp.zeros((PART, GRID), F32)
        downward = jnp.zeros((PART, GRID), F32)
        for step in range(STOPS + 1):
            partner = spec_in[part, step]
            if step < STOPS:
                direct = direct + gains[step] * partner
            if step >= 1:
                upward = upward + (weights[step - 1] * marks_up[step - 1]) * partner
            if step + 1 < STOPS:
                downward = downward + (weights[step + 1] * marks_down[step + 1]) * partner
        mixed = mm3(
            split(jnp.concatenate([direct, upward, downward], axis=0)),
            (from_cols[0][...], from_cols[1][...]),
        )
        smooth = encounter(mixed)
        sine = sines[pl.ds(pl.multiple_of(PAIR * (HALVES * chip + part), PAIR), PAIR), :]
        sine = jnp.concatenate([sine, sine], axis=1)
        along_x = jnp.concatenate([-sine * smooth[PAIR:], sine * smooth[:PAIR]], axis=0)
        along_y = encounter(-0.5 * (pltpu.roll(mixed, GRID - 1, 1) - pltpu.roll(mixed, 1, 1)))
        return jnp.concatenate([along_x, along_y], axis=1).astype(BF16)

    gathers = [[] for _ in range(HALVES)]
    for part in range(HALVES):
        for copy in spectra[part]:
            copy.wait_recv()
        mine = pl.ds(pl.multiple_of(HALF * part + PART * chip, PART), PART)
        total[mine, :] = collect(part)
        for place in range(CHIPS - 1):
            if part == 0:
                step = RING_ORDER[place]
                there = ring(step)[0]
            else:
                there = place + jnp.where(place >= chip, 1, 0)
                step = lax.rem(there - chip + CHIPS, CHIPS)
            copy = pltpu.make_async_remote_copy(
                src_ref=total.at[mine],
                dst_ref=total.at[mine],
                send_sem=total_send.at[part, place],
                recv_sem=total_recv.at[part, step],
                device_id=(bunch, 2 * there + core),
                device_id_type=MESH,
            )
            copy.start()
            gathers[part].append(copy)
    def kicks(part, half, target):
        span = slice(HALF * part, HALF * (part + 1))
        stacked = jnp.concatenate([total[span, :GRID], total[span, GRID:]], axis=0)
        for first in range(0, parts, CHUNK):
            here = pl.ds(half * parts + first, CHUNK)
            values = mm(stacked, col_plain[:, here])
            wave = row_wave[span, here]
            for axis in range(2):
                picked = values[axis * HALF : (axis + 1) * HALF] * wave
                target(half, axis, first, jnp.sum(picked, axis=0, keepdims=True))

    def arrive(part):
        mine = pl.ds(pl.multiple_of(HALF * part + PART * chip, PART), PART)
        for step in range(1, CHIPS):
            pltpu.make_async_remote_copy(
                src_ref=total.at[mine],
                dst_ref=total.at[mine],
                send_sem=total_send.at[part, 0],
                recv_sem=total_recv.at[part, step],
                device_id=ring(step)[1],
                device_id_type=MESH,
            ).wait_recv()

    def keep(half, axis, first, value):
        kick_first[half, axis : axis + 1, first : first + CHUNK] = value

    def to_sibling(half, axis, first, value):
        before = kick_first[half, axis : axis + 1, first : first + CHUNK]
        kick_out[axis : axis + 1, first : first + CHUNK] = before + value

    def to_output(half, axis, first, value):
        before = kick_first[half, axis : axis + 1, first : first + CHUNK]
        kick_own[axis : axis + 1, first : first + CHUNK] = before + value

    arrive(0)
    kicks(0, 1, keep)
    kicks(0, 0, keep)
    arrive(1)
    kicks(1, 1, to_sibling)
    back = pltpu.make_async_remote_copy(
        src_ref=kick_out,
        dst_ref=out_ref.at[core, 0],
        send_sem=kick_send,
        recv_sem=kick_recv,
        device_id=sibling,
        device_id_type=MESH,
    )
    back.start()
    kicks(1, 0, to_output)
    here = pltpu.make_async_copy(kick_own, out_ref.at[core, 0], own_sem)
    here.start()
    here.wait()
    back.wait_recv()
    for copy in [*swaps, *packs, *sums[0], *sums[1], *spectra[0], *spectra[1], *gathers[0], *gathers[1], back]:
        copy.wait_send()


def body(bunches, tables, *operands):
    cell_index, charges, momenta, fill_pattern, encounters, green_spectrum, stop_gain, parasitic_gain = operands
    parts = cell_index.shape[3]
    stacked, sines = tables
    charges = charges.reshape(2, parts)
    fill_pattern = fill_pattern.reshape(2)
    encounters = encounters.reshape(STOPS, 2, 2).transpose(1, 2, 0).reshape(4, STOPS)
    green_spectrum = green_spectrum.T
    operands = (cell_index, charges, fill_pattern, encounters, green_spectrum, stop_gain, parasitic_gain)
    any_spec = pl.BlockSpec(memory_space=pltpu.HBM)
    dma = pltpu.SemaphoreType.DMA
    kicks = pl.pallas_call(
        functools.partial(kernel, bunches),
        out_shape=jax.ShapeDtypeStruct(momenta.shape, F32),
        in_specs=[any_spec] * 9,
        out_specs=any_spec,
        scratch_shapes=[
            pltpu.VMEM((2, 2, parts), jnp.int32),
            pltpu.VMEM((2, parts), BF16),
            pltpu.VMEM((2, parts), BF16),
            pltpu.SMEM(fill_pattern.shape, jnp.int32),
            pltpu.SMEM(encounters.shape, jnp.int32),
            pltpu.VMEM(green_spectrum.shape, F32),
            pltpu.SMEM(stop_gain.shape, F32),
            pltpu.SMEM(parasitic_gain.shape, F32),
            pltpu.VMEM(stacked.shape, BF16),
            pltpu.VMEM(sines.shape, F32),
            pltpu.VMEM((128, GRID), F32),
            pltpu.VMEM((CHIPS, 8, 128), F32),
            pltpu.VMEM((CHIPS, 8, 128), F32),
            pltpu.VMEM((CHIPS, 8, 128), F32),
            pltpu.VMEM((CHIPS, 8, 128), F32),
            pltpu.VMEM((GRID, 2 * parts), BF16),
            pltpu.VMEM((GRID, 2 * parts), BF16),
            pltpu.VMEM((GRID, 2 * parts), BF16),
            pltpu.VMEM((GRID, 2 * parts), F32),
            pltpu.VMEM((2, 2, parts), F32),
            pltpu.VMEM((GRID, GRID), BF16),
            pltpu.VMEM((HALVES, CHIPS, PART, GRID), BF16),
            pltpu.VMEM((HALVES, PART, GRID), F32),
            pltpu.VMEM((HALVES, STOPS + 1, PART, GRID), F32),
            pltpu.VMEM((GRID, 2 * GRID), BF16),
            pltpu.VMEM((2, parts), F32),
            pltpu.VMEM((2, parts), F32),
            dma((9,)),
            dma((3,)),
            dma((3,)),
            dma((CHIPS,)),
            dma((CHIPS,)),
            dma((HALVES, CHIPS)),
            dma((HALVES, CHIPS)),
            dma((HALVES, STOPS + 1)),
            dma((HALVES, STOPS + 1)),
            dma((HALVES, CHIPS)),
            dma((HALVES, CHIPS)),
            dma(()),
            dma(()),
            dma(()),
            pltpu.SemaphoreType.REGULAR,
            pltpu.SemaphoreType.REGULAR,
        ],
        compiler_params=pltpu.CompilerParams(
            collective_id=0, has_side_effects=True, vmem_limit_bytes=60 << 20
        ),
    )(*operands, stacked, sines)
    return momenta + kicks


def solution(mesh):
    in_specs = (
        P(None, "bunch", None, "tile"),
        P(None, "bunch", "tile"),
        P(None, "bunch", None, "tile"),
        P(None, "bunch"),
        P(None, None, None, "bunch"),
        P(None, "tile"),
        P(),
        P(),
    )
    out_specs = P(None, "bunch", None, "tile")
    tables = make_tables()
    return jax.shard_map(
        functools.partial(body, mesh.shape["bunch"], tables),
        mesh=mesh,
        in_specs=in_specs,
        out_specs=out_specs,
        check_vma=False,
    )
```

```python
import functools
import math

import jax
import jax.numpy as jnp
import ml_dtypes
import numpy as np
from jax import lax
from jax.experimental import pallas as pl
from jax.experimental.pallas import tpu as pltpu
from jax.sharding import PartitionSpec as P

GRID = 256
HALF = GRID // 2
STOPS = 4
OFFSET_CELLS = 32
CHIPS = 8
SLAB = GRID // CHIPS
HALVES = 2
PART = SLAB // HALVES
PAIR = PART // 2
CHUNK = 256
LEAD = 4
MESH = pl.DeviceIdType.MESH
F32 = jnp.float32
BF16 = jnp.bfloat16
RING_ORDER = (4, 3, 5, 2, 6, 1, 7)


def split_np(table):
    high = table.astype(ml_dtypes.bfloat16)
    low = (table - high.astype(np.float64)).astype(ml_dtypes.bfloat16)
    return high, low


def basis_rows(wave, is_sine):
    positions = np.arange(GRID)
    if is_sine and wave == 0:
        return np.cos(math.pi * positions) / 16.0
    if wave == 0:
        return np.full(GRID, 1.0 / 16.0)
    angle = 2.0 * math.pi / GRID * ((wave * positions) % GRID)
    return (np.sin(angle) if is_sine else np.cos(angle)) * math.sqrt(2.0) / 16.0


def fold_row(wave, is_sine):
    row = np.zeros(GRID)
    if wave == 0:
        row[HALF if is_sine else 0] = 1.0
    else:
        row[wave] = 0.5
        row[GRID - wave] = -0.5 if is_sine else 0.5
    return row


def make_tables():
    slab_order = [
        (PAIR * part + r % PAIR, r >= PAIR) for part in range(CHIPS * HALVES) for r in range(PART)
    ]
    half_order = [
        slab_order[SLAB * chip + PART * part + r]
        for part in range(HALVES)
        for chip in range(CHIPS)
        for r in range(PART)
    ]
    plain_order = [(q % HALF, q >= HALF) for q in range(GRID)]
    row_basis = np.stack([basis_rows(*entry) for entry in half_order])
    col_basis = np.stack([basis_rows(*entry) for entry in plain_order])
    row_fold = np.stack([fold_row(*entry) for entry in slab_order])
    col_fold = np.stack([fold_row(*entry) for entry in plain_order]).T
    stacked = np.stack(
        [
            *split_np(row_basis),
            *split_np(col_basis.T),
            *split_np(col_basis),
            row_fold.astype(ml_dtypes.bfloat16),
            col_fold.astype(ml_dtypes.bfloat16),
        ]
    )
    sines = np.sin(2.0 * math.pi / GRID * np.arange(HALF))
    return stacked, np.repeat(sines[:, None], 128, axis=1).astype(np.float32)


def split(value):
    high = value.astype(BF16)
    return high, (value - high.astype(F32)).astype(BF16)


def mm(a, b):
    return jnp.dot(a, b, preferred_element_type=F32)


def mm_nt(a, b):
    return lax.dot_general(a, b, (((1,), (1,)), ((), ())), preferred_element_type=F32)


def mm3(a, b):
    return mm(a[0], b[0]) + (mm(a[0], b[1]) + mm(a[1], b[0]))


def kernel(
    bunches,
    cell_ref,
    charge_ref,
    fill_ref,
    mark_ref,
    green_ref,
    stop_ref,
    para_ref,
    table_ref,
    sine_ref,
    out_ref,
    cells,
    charge,
    charge_other,
    fill,
    marks,
    green,
    stop,
    para,
    table,
    sines,
    wide,
    pack_mine,
    pack_other,
    pack_out,
    pack_in,
    row_hot,
    col_hot,
    col_plain,
    row_wave,
    kick_first,
    rows_out,
    rows_in,
    spec_out,
    spec_in,
    total,
    kick_out,
    kick_own,
    load_sem,
    swap_send,
    swap_recv,
    pack_send,
    pack_recv,
    rows_send,
    rows_recv,
    spec_send,
    spec_recv,
    total_send,
    total_recv,
    kick_send,
    kick_recv,
    own_sem,
    ring_in,
    met_in,
):
    parts = cells.shape[2]
    bunch = lax.axis_index("bunch")
    tile = lax.axis_index("tile")
    chip = lax.div(tile, 2)
    core = lax.rem(tile, 2)
    other = 1 - core
    sibling = (bunch, 2 * chip + other)

    def ring(step):
        there = lax.rem(chip + step, CHIPS)
        return there, (bunch, 2 * there + core)

    def meets(step):
        return (lax.rem(bunch + (1 - 2 * core) * step + 4 * bunches, bunches), 2 * chip + other)

    barrier = pltpu.get_barrier_semaphore()
    leads = lax.rem(chip, LEAD) == 0
    near = [sibling] + [ring(step)[1] for step in range(1, CHIPS)]
    for partner in near:
        pl.semaphore_signal(barrier, inc=1, device_id=partner, device_id_type=MESH)

    @pl.when(leads)
    def _():
        for step in range(1, STOPS + 1):
            pl.semaphore_signal(barrier, inc=1, device_id=meets(step), device_id_type=MESH)

    loads = [
        pltpu.make_async_copy(source, target, load_sem.at[index])
        for index, (source, target) in enumerate(
            [
                (green_ref, green),
                (table_ref, table),
                (cell_ref.at[core, 0], cells.at[0]),
                (charge_ref, charge),
                (fill_ref, fill),
                (mark_ref, marks),
                (stop_ref, stop),
                (para_ref, para),
                (sine_ref, sines),
            ]
        )
    ]
    for load in loads:
        load.start()

    row_basis = (table.at[0], table.at[1])
    to_cols = (table.at[2], table.at[3])
    from_cols = (table.at[4], table.at[5])

    loads[0].wait()
    loads[1].wait()
    wide[...] = jnp.zeros(wide.shape, F32)
    wide[0 : green.shape[0]] = green[...]
    green_high, green_low = split(wide[...])
    folded = mm_nt(table[6], green_high) + mm_nt(table[6], green_low)
    folded = folded.reshape(CHIPS, 4, 8, 128)
    packed = folded[:, 0].reshape(CHIPS * 8, 128)
    for group in range(1, 4):
        packed = packed + pltpu.roll(folded[:, group].reshape(CHIPS * 8, 128), 32 * group, 1)
    packed = pltpu.roll(packed, 16 * core, 1)
    pack_mine[...] = packed.reshape(CHIPS, 8, 128)

    pl.semaphore_wait(barrier, jnp.where(leads, len(near) + STOPS, len(near)))

    @pl.when(leads)
    def _():
        for step in range(1, STOPS + 1):
            pl.semaphore_signal(ring_in, inc=1, device_id=meets(step), device_id_type=MESH)

    swaps = [
        pltpu.make_async_remote_copy(
            src_ref=source,
            dst_ref=target,
            send_sem=swap_send.at[index],
            recv_sem=swap_recv.at[index],
            device_id=sibling,
            device_id_type=MESH,
        )
        for index, (source, target) in enumerate(
            [
                (cell_ref.at[other, 0], cells.at[1]),
                (charge_ref, charge_other),
                (pack_mine, pack_other),
            ]
        )
    ]
    for swap in swaps:
        swap.start()

    cell_iota = lax.broadcasted_iota(jnp.int32, (GRID, CHUNK), 0)

    def deposit(half):
        filled = fill[core].astype(F32)
        held = jnp.zeros((1, CHUNK), F32)
        for first in range(0, parts, CHUNK):
            here = pl.ds(half * parts + first, CHUNK)
            rows = cells[half, 0:1, first : first + CHUNK]
            cols = cells[half, 1:2, first : first + CHUNK]
            both = (charge, charge_other)[half][:, first : first + CHUNK].astype(F32)
            weight = jnp.where(core == 0, both[0:1], both[1:2]) * filled
            held = held + weight
            row_hot[:, here] = jnp.where(cell_iota == rows, 1.0, 0.0).astype(BF16)
            col_hot[:, here] = jnp.where(cell_iota == cols, weight, 0.0).astype(BF16)
        span = pl.ds(half * parts, parts)
        return mm_nt(row_hot[:, span], col_hot[:, span]), held

    for load in loads[2:]:
        load.wait()
    density, held = deposit(0)
    for swap in swaps:
        swap.wait_recv()

    pack_out[...] = pack_mine[...] + pack_other[...]
    pack_in[chip] = pack_out[chip]
    packs = []
    for step in RING_ORDER:
        there, device = ring(step)
        copy = pltpu.make_async_remote_copy(
            src_ref=pack_out.at[there],
            dst_ref=pack_in.at[chip],
            send_sem=pack_send.at[step],
            recv_sem=pack_recv.at[step],
            device_id=device,
            device_id_type=MESH,
        )
        copy.start()
        packs.append(copy)

    density_more, held_more = deposit(1)
    density = density + density_more
    level = jnp.sum(held + held_more, axis=1, keepdims=True) * (1.0 / (16.0 * GRID))
    basis_high, basis_low = row_basis[0][...], row_basis[1][...]
    pieces = split(density)
    partial = mm3((basis_high[:HALF], basis_low[:HALF]), pieces)
    rows_out[:HALF, :] = partial.astype(BF16)
    top = partial[0:16]
    first_row = lax.broadcasted_iota(jnp.int32, top.shape, 0) == 0
    rows_out[0:16, :] = jnp.where(first_row, top - level, top).astype(BF16)
    sums = [[] for _ in range(HALVES)]
    for part in range(HALVES):
        if part == 1:
            rows_out[HALF:, :] = mm3((basis_high[HALF:], basis_low[HALF:]), pieces).astype(BF16)
        for step in RING_ORDER:
            there, device = ring(step)
            first = pl.multiple_of(HALF * part + PART * there, PART)
            copy = pltpu.make_async_remote_copy(
                src_ref=rows_out.at[pl.ds(first, PART)],
                dst_ref=rows_in.at[part, step],
                send_sem=rows_send.at[part, step],
                recv_sem=rows_recv.at[part, step],
                device_id=device,
                device_id_type=MESH,
            )
            copy.start()
            sums[part].append(copy)

    for first in range(0, 2 * parts, CHUNK):
        here = pl.ds(first, CHUNK)
        row_wave[:, here] = mm(basis_high, row_hot[:, here]) + mm(basis_low, row_hot[:, here])
        cols = cells[first // parts, 1:2, first % parts : first % parts + CHUNK]
        col_plain[:, here] = jnp.where(cell_iota == cols, 1.0, 0.0).astype(BF16)

    @pl.when(leads)
    def _():
        pl.semaphore_wait(ring_in, STOPS)
        for ahead in range(1, LEAD):
            follower = (bunch, 2 * (chip + ahead) + core)
            pl.semaphore_signal(met_in, inc=1, device_id=follower, device_id_type=MESH)

    for copy in packs:
        copy.wait_recv()
    lane = lax.broadcasted_iota(jnp.int32, (8, 128), 1)
    halves = []
    for side in range(2):
        groups = []
        for group in range(4):
            merged = jnp.zeros((8, 128), F32)
            for spot in range(4):
                moved = pack_in[4 * side + spot]
                shift = (32 * (spot - group)) % 128
                if shift:
                    moved = pltpu.roll(moved, shift, 1)
                merged = jnp.where(lane // 32 == spot, moved, merged)
            groups.append(merged)
        halves.append(jnp.concatenate(groups, axis=0))
    slab_high, slab_low = split(jnp.concatenate(halves, axis=1))
    factors = mm(slab_high, table[7]) + mm(slab_low, table[7])
    lanes = lax.broadcasted_iota(jnp.int32, (PAIR, HALF), 1)
    subs = lax.broadcasted_iota(jnp.int32, (PAIR, HALF), 0)

    def convolve(part):
        even = factors[PART * part : PART * part + PAIR]
        odd = factors[PART * part + PAIR : PART * (part + 1)]
        gain_cc = even[:, :HALF]
        gain_cs = jnp.where(lanes == 0, even[:, HALF:], gain_cc)
        gain_sc, gain_ss, edge = gain_cc, gain_cs, lanes == 0
        if part == 0:
            special = jnp.logical_and(subs == 0, chip == 0)
            gain_sc = jnp.where(special, odd[:, :HALF], gain_cc)
            gain_ss = jnp.where(special, jnp.where(lanes == 0, odd[:, HALF:], odd[:, :HALF]), gain_cs)
            edge = jnp.logical_or(special, lanes == 0)
        mixing = jnp.where(edge, 0.0, odd[:, HALF:])
        slab = rows_out[pl.ds(pl.multiple_of(HALF * part + PART * chip, PART), PART), :].astype(F32)
        for step in range(1, CHIPS):
            slab = slab + rows_in[part, step].astype(F32)
        spectrum = mm3(split(slab), (to_cols[0][...], to_cols[1][...]))
        part_cc, part_cs = spectrum[:PAIR, :HALF], spectrum[:PAIR, HALF:]
        part_sc, part_ss = spectrum[PAIR:, :HALF], spectrum[PAIR:, HALF:]
        spec_out[part, :PAIR, :HALF] = gain_cc * part_cc - mixing * part_ss
        spec_out[part, :PAIR, HALF:] = gain_cs * part_cs + mixing * part_sc
        spec_out[part, PAIR:, :HALF] = gain_sc * part_sc + mixing * part_cs
        spec_out[part, PAIR:, HALF:] = gain_ss * part_ss - mixing * part_cc

    spectra = [[] for _ in range(HALVES)]
    for part in range(HALVES):
        for copy in sums[part]:
            copy.wait_recv()
        convolve(part)
        if part == 0:

            @pl.when(jnp.logical_not(leads))
            def _():
                pl.semaphore_wait(met_in, 1)

        for step in (4, 3, 2, 1, 0):
            copy = pltpu.make_async_remote_copy(
                src_ref=spec_out.at[part],
                dst_ref=spec_in.at[part, step],
                send_sem=spec_send.at[part, step],
                recv_sem=spec_recv.at[part, step],
                device_id=meets(step),
                device_id_type=MESH,
            )
            copy.start()
            spectra[part].append(copy)

    gains = [stop[s] for s in range(STOPS)]
    weights = [stop[s] * para[s] for s in range(STOPS)]
    marks_up = [marks[2 * core, s].astype(F32) for s in range(STOPS)]
    marks_down = [marks[2 * core + 1, s].astype(F32) for s in range(STOPS)]
    column = lax.broadcasted_iota(jnp.int32, (PART, GRID), 1)

    def encounter(three):
        moved_up = jnp.where(column >= OFFSET_CELLS, pltpu.roll(three[PART : 2 * PART], OFFSET_CELLS, 1), 0.0)
        moved_down = jnp.where(
            column < GRID - OFFSET_CELLS, pltpu.roll(three[2 * PART :], GRID - OFFSET_CELLS, 1), 0.0
        )
        return three[:PART] + moved_up + moved_down

    def collect(part):
        direct = jnp.zeros((PART, GRID), F32)
        upward = jnp.zeros((PART, GRID), F32)
        downward = jnp.zeros((PART, GRID), F32)
        for step in range(STOPS + 1):
            partner = spec_in[part, step]
            if step < STOPS:
                direct = direct + gains[step] * partner
            if step >= 1:
                upward = upward + (weights[step - 1] * marks_up[step - 1]) * partner
            if step + 1 < STOPS:
                downward = downward + (weights[step + 1] * marks_down[step + 1]) * partner
        mixed = mm3(
            split(jnp.concatenate([direct, upward, downward], axis=0)),
            (from_cols[0][...], from_cols[1][...]),
        )
        smooth = encounter(mixed)
        sine = sines[pl.ds(pl.multiple_of(PAIR * (HALVES * chip + part), PAIR), PAIR), :]
        sine = jnp.concatenate([sine, sine], axis=1)
        along_x = jnp.concatenate([-sine * smooth[PAIR:], sine * smooth[:PAIR]], axis=0)
        along_y = encounter(-0.5 * (pltpu.roll(mixed, GRID - 1, 1) - pltpu.roll(mixed, 1, 1)))
        return jnp.concatenate([along_x, along_y], axis=1).astype(BF16)

    gathers = [[] for _ in range(HALVES)]
    for part in range(HALVES):
        for copy in spectra[part]:
            copy.wait_recv()
        mine = pl.ds(pl.multiple_of(HALF * part + PART * chip, PART), PART)
        total[mine, :] = collect(part)
        for place in range(CHIPS - 1):
            if part == 0:
                step = RING_ORDER[place]
                there = ring(step)[0]
            else:
                there = place + jnp.where(place >= chip, 1, 0)
                step = lax.rem(there - chip + CHIPS, CHIPS)
            copy = pltpu.make_async_remote_copy(
                src_ref=total.at[mine],
                dst_ref=total.at[mine],
                send_sem=total_send.at[part, place],
                recv_sem=total_recv.at[part, step],
                device_id=(bunch, 2 * there + core),
                device_id_type=MESH,
            )
            copy.start()
            gathers[part].append(copy)
    def kicks(part, half, target):
        span = slice(HALF * part, HALF * (part + 1))
        stacked = jnp.concatenate([total[span, :GRID], total[span, GRID:]], axis=0)
        for first in range(0, parts, CHUNK):
            here = pl.ds(half * parts + first, CHUNK)
            values = mm(stacked, col_plain[:, here])
            wave = row_wave[span, here]
            for axis in range(2):
                picked = values[axis * HALF : (axis + 1) * HALF] * wave
                target(half, axis, first, jnp.sum(picked, axis=0, keepdims=True))

    def arrive(part):
        mine = pl.ds(pl.multiple_of(HALF * part + PART * chip, PART), PART)
        for step in range(1, CHIPS):
            pltpu.make_async_remote_copy(
                src_ref=total.at[mine],
                dst_ref=total.at[mine],
                send_sem=total_send.at[part, 0],
                recv_sem=total_recv.at[part, step],
                device_id=ring(step)[1],
                device_id_type=MESH,
            ).wait_recv()

    def keep(half, axis, first, value):
        kick_first[half, axis : axis + 1, first : first + CHUNK] = value

    def to_sibling(half, axis, first, value):
        before = kick_first[half, axis : axis + 1, first : first + CHUNK]
        kick_out[axis : axis + 1, first : first + CHUNK] = before + value

    def to_output(half, axis, first, value):
        before = kick_first[half, axis : axis + 1, first : first + CHUNK]
        kick_own[axis : axis + 1, first : first + CHUNK] = before + value

    arrive(0)
    kicks(0, 1, keep)
    kicks(0, 0, keep)
    arrive(1)
    kicks(1, 1, to_sibling)
    back = pltpu.make_async_remote_copy(
        src_ref=kick_out,
        dst_ref=out_ref.at[core, 0],
        send_sem=kick_send,
        recv_sem=kick_recv,
        device_id=sibling,
        device_id_type=MESH,
    )
    back.start()
    kicks(1, 0, to_output)
    here = pltpu.make_async_copy(kick_own, out_ref.at[core, 0], own_sem)
    here.start()
    here.wait()
    back.wait_recv()
    for copy in [*swaps, *packs, *sums[0], *sums[1], *spectra[0], *spectra[1], *gathers[0], *gathers[1], back]:
        copy.wait_send()


def body(bunches, tables, *operands):
    cell_index, charges, momenta, fill_pattern, encounters, green_spectrum, stop_gain, parasitic_gain = operands
    parts = cell_index.shape[3]
    stacked, sines = tables
    charges = charges.reshape(2, parts)
    fill_pattern = fill_pattern.reshape(2)
    encounters = encounters.reshape(STOPS, 2, 2).transpose(1, 2, 0).reshape(4, STOPS)
    green_spectrum = green_spectrum.T
    operands = (cell_index, charges, fill_pattern, encounters, green_spectrum, stop_gain, parasitic_gain)
    any_spec = pl.BlockSpec(memory_space=pltpu.HBM)
    dma = pltpu.SemaphoreType.DMA
    kicks = pl.pallas_call(
        functools.partial(kernel, bunches),
        out_shape=jax.ShapeDtypeStruct(momenta.shape, F32),
        in_specs=[any_spec] * 9,
        out_specs=any_spec,
        scratch_shapes=[
            pltpu.VMEM((2, 2, parts), jnp.int32),
            pltpu.VMEM((2, parts), BF16),
            pltpu.VMEM((2, parts), BF16),
            pltpu.SMEM(fill_pattern.shape, jnp.int32),
            pltpu.SMEM(encounters.shape, jnp.int32),
            pltpu.VMEM(green_spectrum.shape, F32),
            pltpu.SMEM(stop_gain.shape, F32),
            pltpu.SMEM(parasitic_gain.shape, F32),
            pltpu.VMEM(stacked.shape, BF16),
            pltpu.VMEM(sines.shape, F32),
            pltpu.VMEM((128, GRID), F32),
            pltpu.VMEM((CHIPS, 8, 128), F32),
            pltpu.VMEM((CHIPS, 8, 128), F32),
            pltpu.VMEM((CHIPS, 8, 128), F32),
            pltpu.VMEM((CHIPS, 8, 128), F32),
            pltpu.VMEM((GRID, 2 * parts), BF16),
            pltpu.VMEM((GRID, 2 * parts), BF16),
            pltpu.VMEM((GRID, 2 * parts), BF16),
            pltpu.VMEM((GRID, 2 * parts), F32),
            pltpu.VMEM((2, 2, parts), F32),
            pltpu.VMEM((GRID, GRID), BF16),
            pltpu.VMEM((HALVES, CHIPS, PART, GRID), BF16),
            pltpu.VMEM((HALVES, PART, GRID), F32),
            pltpu.VMEM((HALVES, STOPS + 1, PART, GRID), F32),
            pltpu.VMEM((GRID, 2 * GRID), BF16),
            pltpu.VMEM((2, parts), F32),
            pltpu.VMEM((2, parts), F32),
            dma((9,)),
            dma((3,)),
            dma((3,)),
            dma((CHIPS,)),
            dma((CHIPS,)),
            dma((HALVES, CHIPS)),
            dma((HALVES, CHIPS)),
            dma((HALVES, STOPS + 1)),
            dma((HALVES, STOPS + 1)),
            dma((HALVES, CHIPS)),
            dma((HALVES, CHIPS)),
            dma(()),
            dma(()),
            dma(()),
            pltpu.SemaphoreType.REGULAR,
            pltpu.SemaphoreType.REGULAR,
        ],
        compiler_params=pltpu.CompilerParams(
            collective_id=0, has_side_effects=True, vmem_limit_bytes=60 << 20
        ),
    )(*operands, stacked, sines)
    return momenta + kicks


def solution(mesh):
    in_specs = (
        P(None, "bunch", None, "tile"),
        P(None, "bunch", "tile"),
        P(None, "bunch", None, "tile"),
        P(None, "bunch"),
        P(None, None, None, "bunch"),
        P(None, "tile"),
        P(),
        P(),
    )
    out_specs = P(None, "bunch", None, "tile")
    tables = make_tables()
    return jax.shard_map(
        functools.partial(body, mesh.shape["bunch"], tables),
        mesh=mesh,
        in_specs=in_specs,
        out_specs=out_specs,
        check_vma=False,
    )
```

```python
import functools
import math

import jax
import jax.numpy as jnp
import ml_dtypes
import numpy as np
from jax import lax
from jax.experimental import pallas as pl
from jax.experimental.pallas import tpu as pltpu
from jax.sharding import PartitionSpec as P

GRID = 256
HALF = GRID // 2
STOPS = 4
OFFSET_CELLS = 32
CHIPS = 8
SLAB = GRID // CHIPS
HALVES = 2
PART = SLAB // HALVES
PAIR = PART // 2
CHUNK = 256
LEAD = 4
MESH = pl.DeviceIdType.MESH
F32 = jnp.float32
BF16 = jnp.bfloat16
RING_ORDER = (4, 5, 3, 6, 2, 7, 1)


def split_np(table):
    high = table.astype(ml_dtypes.bfloat16)
    low = (table - high.astype(np.float64)).astype(ml_dtypes.bfloat16)
    return high, low


def basis_rows(wave, is_sine):
    positions = np.arange(GRID)
    if is_sine and wave == 0:
        return np.cos(math.pi * positions) / 16.0
    if wave == 0:
        return np.full(GRID, 1.0 / 16.0)
    angle = 2.0 * math.pi / GRID * ((wave * positions) % GRID)
    return (np.sin(angle) if is_sine else np.cos(angle)) * math.sqrt(2.0) / 16.0


def fold_row(wave, is_sine):
    row = np.zeros(GRID)
    if wave == 0:
        row[HALF if is_sine else 0] = 1.0
    else:
        row[wave] = 0.5
        row[GRID - wave] = -0.5 if is_sine else 0.5
    return row


def make_tables():
    slab_order = [
        (PAIR * part + r % PAIR, r >= PAIR) for part in range(CHIPS * HALVES) for r in range(PART)
    ]
    half_order = [
        slab_order[SLAB * chip + PART * part + r]
        for part in range(HALVES)
        for chip in range(CHIPS)
        for r in range(PART)
    ]
    plain_order = [(q % HALF, q >= HALF) for q in range(GRID)]
    row_basis = np.stack([basis_rows(*entry) for entry in half_order])
    col_basis = np.stack([basis_rows(*entry) for entry in plain_order])
    row_fold = np.stack([fold_row(*entry) for entry in slab_order])
    col_fold = np.stack([fold_row(*entry) for entry in plain_order]).T
    stacked = np.stack(
        [
            *split_np(row_basis),
            *split_np(col_basis.T),
            *split_np(col_basis),
            row_fold.astype(ml_dtypes.bfloat16),
            col_fold.astype(ml_dtypes.bfloat16),
        ]
    )
    sines = np.sin(2.0 * math.pi / GRID * np.arange(HALF))
    return stacked, np.repeat(sines[:, None], 128, axis=1).astype(np.float32)


def split(value):
    high = value.astype(BF16)
    return high, (value - high.astype(F32)).astype(BF16)


def mm(a, b):
    return jnp.dot(a, b, preferred_element_type=F32)


def mm_nt(a, b):
    return lax.dot_general(a, b, (((1,), (1,)), ((), ())), preferred_element_type=F32)


def mm3(a, b):
    return mm(a[0], b[0]) + (mm(a[0], b[1]) + mm(a[1], b[0]))


def kernel(
    bunches,
    cell_ref,
    charge_ref,
    fill_ref,
    mark_ref,
    green_ref,
    stop_ref,
    para_ref,
    table_ref,
    sine_ref,
    out_ref,
    cells,
    charge,
    charge_other,
    fill,
    marks,
    green,
    stop,
    para,
    table,
    sines,
    wide,
    pack_mine,
    pack_other,
    pack_out,
    pack_in,
    row_hot,
    col_hot,
    col_plain,
    row_wave,
    kick_first,
    rows_out,
    rows_in,
    spec_out,
    spec_in,
    total,
    kick_out,
    kick_own,
    load_sem,
    swap_send,
    swap_recv,
    pack_send,
    pack_recv,
    rows_send,
    rows_recv,
    spec_send,
    spec_recv,
    total_send,
    total_recv,
    kick_send,
    kick_recv,
    own_sem,
    ring_in,
    met_in,
):
    parts = cells.shape[2]
    bunch = lax.axis_index("bunch")
    tile = lax.axis_index("tile")
    chip = lax.div(tile, 2)
    core = lax.rem(tile, 2)
    other = 1 - core
    sibling = (bunch, 2 * chip + other)

    def ring(step):
        there = lax.rem(chip + step, CHIPS)
        return there, (bunch, 2 * there + core)

    def meets(step):
        return (lax.rem(bunch + (1 - 2 * core) * step + 4 * bunches, bunches), 2 * chip + other)

    barrier = pltpu.get_barrier_semaphore()
    leads = lax.rem(chip, LEAD) == 0
    near = [sibling] + [ring(step)[1] for step in range(1, CHIPS)]
    for partner in near:
        pl.semaphore_signal(barrier, inc=1, device_id=partner, device_id_type=MESH)

    @pl.when(leads)
    def _():
        for step in range(1, STOPS + 1):
            pl.semaphore_signal(barrier, inc=1, device_id=meets(step), device_id_type=MESH)

    loads = [
        pltpu.make_async_copy(source, target, load_sem.at[index])
        for index, (source, target) in enumerate(
            [
                (green_ref, green),
                (table_ref, table),
                (cell_ref.at[core, 0], cells.at[0]),
                (charge_ref, charge),
                (fill_ref, fill),
                (mark_ref, marks),
                (stop_ref, stop),
                (para_ref, para),
                (sine_ref, sines),
            ]
        )
    ]
    for load in loads:
        load.start()

    row_basis = (table.at[0], table.at[1])
    to_cols = (table.at[2], table.at[3])
    from_cols = (table.at[4], table.at[5])

    loads[0].wait()
    loads[1].wait()
    wide[...] = jnp.zeros(wide.shape, F32)
    wide[0 : green.shape[0]] = green[...]
    green_high, green_low = split(wide[...])
    folded = mm_nt(table[6], green_high) + mm_nt(table[6], green_low)
    folded = folded.reshape(CHIPS, 4, 8, 128)
    packed = folded[:, 0].reshape(CHIPS * 8, 128)
    for group in range(1, 4):
        packed = packed + pltpu.roll(folded[:, group].reshape(CHIPS * 8, 128), 32 * group, 1)
    packed = pltpu.roll(packed, 16 * core, 1)
    pack_mine[...] = packed.reshape(CHIPS, 8, 128)

    pl.semaphore_wait(barrier, jnp.where(leads, len(near) + STOPS, len(near)))

    @pl.when(leads)
    def _():
        for step in range(1, STOPS + 1):
            pl.semaphore_signal(ring_in, inc=1, device_id=meets(step), device_id_type=MESH)

    swaps = [
        pltpu.make_async_remote_copy(
            src_ref=source,
            dst_ref=target,
            send_sem=swap_send.at[index],
            recv_sem=swap_recv.at[index],
            device_id=sibling,
            device_id_type=MESH,
        )
        for index, (source, target) in enumerate(
            [
                (cell_ref.at[other, 0], cells.at[1]),
                (charge_ref, charge_other),
                (pack_mine, pack_other),
            ]
        )
    ]
    for swap in swaps:
        swap.start()

    cell_iota = lax.broadcasted_iota(jnp.int32, (GRID, CHUNK), 0)

    def deposit(half):
        filled = fill[core].astype(F32)
        for first in range(0, parts, CHUNK):
            here = pl.ds(half * parts + first, CHUNK)
            rows = cells[half, 0:1, first : first + CHUNK]
            cols = cells[half, 1:2, first : first + CHUNK]
            both = (charge, charge_other)[half][:, first : first + CHUNK].astype(F32)
            weight = jnp.where(core == 0, both[0:1], both[1:2]) * filled
            row_hot[:, here] = jnp.where(cell_iota == rows, 1.0, 0.0).astype(BF16)
            col_hot[:, here] = jnp.where(cell_iota == cols, weight, 0.0).astype(BF16)
        span = pl.ds(half * parts, parts)
        return mm_nt(row_hot[:, span], col_hot[:, span])

    for load in loads[2:]:
        load.wait()
    density = deposit(0)
    for swap in swaps:
        swap.wait_recv()

    pack_out[...] = pack_mine[...] + pack_other[...]
    pack_in[chip] = pack_out[chip]
    packs = []
    for step in RING_ORDER:
        there, device = ring(step)
        copy = pltpu.make_async_remote_copy(
            src_ref=pack_out.at[there],
            dst_ref=pack_in.at[chip],
            send_sem=pack_send.at[step],
            recv_sem=pack_recv.at[step],
            device_id=device,
            device_id_type=MESH,
        )
        copy.start()
        packs.append(copy)

    density = density + deposit(1)
    basis_high, basis_low = row_basis[0][...], row_basis[1][...]
    pieces = split(density)
    partial = mm3((basis_high[:HALF], basis_low[:HALF]), pieces)
    rows_out[:HALF, :] = partial.astype(BF16)
    top = partial[0:16]
    first_row = lax.broadcasted_iota(jnp.int32, top.shape, 0) == 0
    rows_out[0:16, :] = jnp.where(first_row, top - jnp.mean(top, axis=1, keepdims=True), top).astype(BF16)
    sums = [[] for _ in range(HALVES)]
    for part in range(HALVES):
        if part == 1:
            rows_out[HALF:, :] = mm3((basis_high[HALF:], basis_low[HALF:]), pieces).astype(BF16)
        for step in RING_ORDER:
            there, device = ring(step)
            first = pl.multiple_of(HALF * part + PART * there, PART)
            copy = pltpu.make_async_remote_copy(
                src_ref=rows_out.at[pl.ds(first, PART)],
                dst_ref=rows_in.at[part, step],
                send_sem=rows_send.at[part, step],
                recv_sem=rows_recv.at[part, step],
                device_id=device,
                device_id_type=MESH,
            )
            copy.start()
            sums[part].append(copy)

    for first in range(0, 2 * parts, CHUNK):
        here = pl.ds(first, CHUNK)
        row_wave[:, here] = mm(basis_high, row_hot[:, here]) + mm(basis_low, row_hot[:, here])
        cols = cells[first // parts, 1:2, first % parts : first % parts + CHUNK]
        col_plain[:, here] = jnp.where(cell_iota == cols, 1.0, 0.0).astype(BF16)

    @pl.when(leads)
    def _():
        pl.semaphore_wait(ring_in, STOPS)
        for ahead in range(1, LEAD):
            follower = (bunch, 2 * (chip + ahead) + core)
            pl.semaphore_signal(met_in, inc=1, device_id=follower, device_id_type=MESH)

    for copy in packs:
        copy.wait_recv()
    lane = lax.broadcasted_iota(jnp.int32, (8, 128), 1)
    halves = []
    for side in range(2):
        groups = []
        for group in range(4):
            merged = jnp.zeros((8, 128), F32)
            for spot in range(4):
                moved = pack_in[4 * side + spot]
                shift = (32 * (spot - group)) % 128
                if shift:
                    moved = pltpu.roll(moved, shift, 1)
                merged = jnp.where(lane // 32 == spot, moved, merged)
            groups.append(merged)
        halves.append(jnp.concatenate(groups, axis=0))
    slab_high, slab_low = split(jnp.concatenate(halves, axis=1))
    factors = mm(slab_high, table[7]) + mm(slab_low, table[7])
    lanes = lax.broadcasted_iota(jnp.int32, (PAIR, HALF), 1)
    subs = lax.broadcasted_iota(jnp.int32, (PAIR, HALF), 0)

    def convolve(part):
        even = factors[PART * part : PART * part + PAIR]
        odd = factors[PART * part + PAIR : PART * (part + 1)]
        gain_cc = even[:, :HALF]
        gain_cs = jnp.where(lanes == 0, even[:, HALF:], gain_cc)
        gain_sc, gain_ss, edge = gain_cc, gain_cs, lanes == 0
        if part == 0:
            special = jnp.logical_and(subs == 0, chip == 0)
            gain_sc = jnp.where(special, odd[:, :HALF], gain_cc)
            gain_ss = jnp.where(special, jnp.where(lanes == 0, odd[:, HALF:], odd[:, :HALF]), gain_cs)
            edge = jnp.logical_or(special, lanes == 0)
        mixing = jnp.where(edge, 0.0, odd[:, HALF:])
        slab = rows_out[pl.ds(pl.multiple_of(HALF * part + PART * chip, PART), PART), :].astype(F32)
        for step in range(1, CHIPS):
            slab = slab + rows_in[part, step].astype(F32)
        spectrum = mm3(split(slab), (to_cols[0][...], to_cols[1][...]))
        part_cc, part_cs = spectrum[:PAIR, :HALF], spectrum[:PAIR, HALF:]
        part_sc, part_ss = spectrum[PAIR:, :HALF], spectrum[PAIR:, HALF:]
        spec_out[part, :PAIR, :HALF] = gain_cc * part_cc - mixing * part_ss
        spec_out[part, :PAIR, HALF:] = gain_cs * part_cs + mixing * part_sc
        spec_out[part, PAIR:, :HALF] = gain_sc * part_sc + mixing * part_cs
        spec_out[part, PAIR:, HALF:] = gain_ss * part_ss - mixing * part_cc

    spectra = [[] for _ in range(HALVES)]
    for part in range(HALVES):
        for copy in sums[part]:
            copy.wait_recv()
        convolve(part)
        if part == 0:

            @pl.when(jnp.logical_not(leads))
            def _():
                pl.semaphore_wait(met_in, 1)

        for step in (4, 3, 2, 1, 0):
            copy = pltpu.make_async_remote_copy(
                src_ref=spec_out.at[part],
                dst_ref=spec_in.at[part, step],
                send_sem=spec_send.at[part, step],
                recv_sem=spec_recv.at[part, step],
                device_id=meets(step),
                device_id_type=MESH,
            )
            copy.start()
            spectra[part].append(copy)

    gains = [stop[s] for s in range(STOPS)]
    weights = [stop[s] * para[s] for s in range(STOPS)]
    marks_up = [marks[2 * core, s].astype(F32) for s in range(STOPS)]
    marks_down = [marks[2 * core + 1, s].astype(F32) for s in range(STOPS)]
    column = lax.broadcasted_iota(jnp.int32, (PART, GRID), 1)

    def encounter(three):
        moved_up = jnp.where(column >= OFFSET_CELLS, pltpu.roll(three[PART : 2 * PART], OFFSET_CELLS, 1), 0.0)
        moved_down = jnp.where(
            column < GRID - OFFSET_CELLS, pltpu.roll(three[2 * PART :], GRID - OFFSET_CELLS, 1), 0.0
        )
        return three[:PART] + moved_up + moved_down

    def collect(part):
        direct = jnp.zeros((PART, GRID), F32)
        upward = jnp.zeros((PART, GRID), F32)
        downward = jnp.zeros((PART, GRID), F32)
        for step in range(STOPS + 1):
            partner = spec_in[part, step]
            if step < STOPS:
                direct = direct + gains[step] * partner
            if step >= 1:
                upward = upward + (weights[step - 1] * marks_up[step - 1]) * partner
            if step + 1 < STOPS:
                downward = downward + (weights[step + 1] * marks_down[step + 1]) * partner
        mixed = mm3(
            split(jnp.concatenate([direct, upward, downward], axis=0)),
            (from_cols[0][...], from_cols[1][...]),
        )
        smooth = encounter(mixed)
        sine = sines[pl.ds(pl.multiple_of(PAIR * (HALVES * chip + part), PAIR), PAIR), :]
        sine = jnp.concatenate([sine, sine], axis=1)
        along_x = jnp.concatenate([-sine * smooth[PAIR:], sine * smooth[:PAIR]], axis=0)
        along_y = encounter(-0.5 * (pltpu.roll(mixed, GRID - 1, 1) - pltpu.roll(mixed, 1, 1)))
        return jnp.concatenate([along_x, along_y], axis=1).astype(BF16)

    gathers = [[] for _ in range(HALVES)]
    for part in range(HALVES):
        for copy in spectra[part]:
            copy.wait_recv()
        mine = pl.ds(pl.multiple_of(HALF * part + PART * chip, PART), PART)
        total[mine, :] = collect(part)
        for place in range(CHIPS - 1):
            if part == 0:
                step = RING_ORDER[place]
                there = ring(step)[0]
            else:
                there = place + jnp.where(place >= chip, 1, 0)
                step = lax.rem(there - chip + CHIPS, CHIPS)
            copy = pltpu.make_async_remote_copy(
                src_ref=total.at[mine],
                dst_ref=total.at[mine],
                send_sem=total_send.at[part, place],
                recv_sem=total_recv.at[part, step],
                device_id=(bunch, 2 * there + core),
                device_id_type=MESH,
            )
            copy.start()
            gathers[part].append(copy)
    def kicks(part, half, target):
        span = slice(HALF * part, HALF * (part + 1))
        stacked = jnp.concatenate([total[span, :GRID], total[span, GRID:]], axis=0)
        for first in range(0, parts, CHUNK):
            here = pl.ds(half * parts + first, CHUNK)
            values = mm(stacked, col_plain[:, here])
            wave = row_wave[span, here]
            for axis in range(2):
                picked = values[axis * HALF : (axis + 1) * HALF] * wave
                target(half, axis, first, jnp.sum(picked, axis=0, keepdims=True))

    def arrive(part):
        mine = pl.ds(pl.multiple_of(HALF * part + PART * chip, PART), PART)
        for step in range(1, CHIPS):
            pltpu.make_async_remote_copy(
                src_ref=total.at[mine],
                dst_ref=total.at[mine],
                send_sem=total_send.at[part, 0],
                recv_sem=total_recv.at[part, step],
                device_id=ring(step)[1],
                device_id_type=MESH,
            ).wait_recv()

    def keep(half, axis, first, value):
        kick_first[half, axis : axis + 1, first : first + CHUNK] = value

    def to_sibling(half, axis, first, value):
        before = kick_first[half, axis : axis + 1, first : first + CHUNK]
        kick_out[axis : axis + 1, first : first + CHUNK] = before + value

    def to_output(half, axis, first, value):
        before = kick_first[half, axis : axis + 1, first : first + CHUNK]
        kick_own[axis : axis + 1, first : first + CHUNK] = before + value

    arrive(0)
    kicks(0, 1, keep)
    kicks(0, 0, keep)
    arrive(1)
    kicks(1, 1, to_sibling)
    back = pltpu.make_async_remote_copy(
        src_ref=kick_out,
        dst_ref=out_ref.at[core, 0],
        send_sem=kick_send,
        recv_sem=kick_recv,
        device_id=sibling,
        device_id_type=MESH,
    )
    back.start()
    kicks(1, 0, to_output)
    here = pltpu.make_async_copy(kick_own, out_ref.at[core, 0], own_sem)
    here.start()
    here.wait()
    back.wait_recv()
    for copy in [*swaps, *packs, *sums[0], *sums[1], *spectra[0], *spectra[1], *gathers[0], *gathers[1], back]:
        copy.wait_send()


def body(bunches, tables, *operands):
    cell_index, charges, momenta, fill_pattern, encounters, green_spectrum, stop_gain, parasitic_gain = operands
    parts = cell_index.shape[3]
    stacked, sines = tables
    charges = charges.reshape(2, parts)
    fill_pattern = fill_pattern.reshape(2)
    encounters = encounters.reshape(STOPS, 2, 2).transpose(1, 2, 0).reshape(4, STOPS)
    green_spectrum = green_spectrum.T
    operands = (cell_index, charges, fill_pattern, encounters, green_spectrum, stop_gain, parasitic_gain)
    any_spec = pl.BlockSpec(memory_space=pltpu.HBM)
    dma = pltpu.SemaphoreType.DMA
    kicks = pl.pallas_call(
        functools.partial(kernel, bunches),
        out_shape=jax.ShapeDtypeStruct(momenta.shape, F32),
        in_specs=[any_spec] * 9,
        out_specs=any_spec,
        scratch_shapes=[
            pltpu.VMEM((2, 2, parts), jnp.int32),
            pltpu.VMEM((2, parts), BF16),
            pltpu.VMEM((2, parts), BF16),
            pltpu.SMEM(fill_pattern.shape, jnp.int32),
            pltpu.SMEM(encounters.shape, jnp.int32),
            pltpu.VMEM(green_spectrum.shape, F32),
            pltpu.SMEM(stop_gain.shape, F32),
            pltpu.SMEM(parasitic_gain.shape, F32),
            pltpu.VMEM(stacked.shape, BF16),
            pltpu.VMEM(sines.shape, F32),
            pltpu.VMEM((128, GRID), F32),
            pltpu.VMEM((CHIPS, 8, 128), F32),
            pltpu.VMEM((CHIPS, 8, 128), F32),
            pltpu.VMEM((CHIPS, 8, 128), F32),
            pltpu.VMEM((CHIPS, 8, 128), F32),
            pltpu.VMEM((GRID, 2 * parts), BF16),
            pltpu.VMEM((GRID, 2 * parts), BF16),
            pltpu.VMEM((GRID, 2 * parts), BF16),
            pltpu.VMEM((GRID, 2 * parts), F32),
            pltpu.VMEM((2, 2, parts), F32),
            pltpu.VMEM((GRID, GRID), BF16),
            pltpu.VMEM((HALVES, CHIPS, PART, GRID), BF16),
            pltpu.VMEM((HALVES, PART, GRID), F32),
            pltpu.VMEM((HALVES, STOPS + 1, PART, GRID), F32),
            pltpu.VMEM((GRID, 2 * GRID), BF16),
            pltpu.VMEM((2, parts), F32),
            pltpu.VMEM((2, parts), F32),
            dma((9,)),
            dma((3,)),
            dma((3,)),
            dma((CHIPS,)),
            dma((CHIPS,)),
            dma((HALVES, CHIPS)),
            dma((HALVES, CHIPS)),
            dma((HALVES, STOPS + 1)),
            dma((HALVES, STOPS + 1)),
            dma((HALVES, CHIPS)),
            dma((HALVES, CHIPS)),
            dma(()),
            dma(()),
            dma(()),
            pltpu.SemaphoreType.REGULAR,
            pltpu.SemaphoreType.REGULAR,
        ],
        compiler_params=pltpu.CompilerParams(
            collective_id=0, has_side_effects=True, vmem_limit_bytes=60 << 20
        ),
    )(*operands, stacked, sines)
    return momenta + kicks


def solution(mesh):
    in_specs = (
        P(None, "bunch", None, "tile"),
        P(None, "bunch", "tile"),
        P(None, "bunch", None, "tile"),
        P(None, "bunch"),
        P(None, None, None, "bunch"),
        P(None, "tile"),
        P(),
        P(),
    )
    out_specs = P(None, "bunch", None, "tile")
    tables = make_tables()
    return jax.shard_map(
        functools.partial(body, mesh.shape["bunch"], tables),
        mesh=mesh,
        in_specs=in_specs,
        out_specs=out_specs,
        check_vma=False,
    )
```
